512 devices in a mesh: row: 8 (over y, x_hi), col: 16 (over z), layer: 4 (over x_lo, core).
Axes of the slice: x: 4 (x_hi: 2, x_lo: 2; x = x_hi * 2 + x_lo), y: 4, z: 16, core: 2. Of those that a mesh axis runs over, the one named last changes fastest.
Arguments:
- density: bfloat16 [2048, 16384], P('row', ('layer', 'col')), may hold values from -6 to 6
- margin: bfloat16 [16384, 16384], P(('layer', 'row'), 'col'), may hold values from -0.09375 to 0.09375
- block_pattern: int32 [128, 128], replicated, may hold values from 0 to 1, as said below
- atom_functions: int32 [512], replicated, may hold values from 1 to 9, 2048 in all
- atom_kind: int32 [512], P(('row', 'col', 'layer')), may hold values from 0 to 4
- atom_offset: float32 [3, 512], P(None, ('row', 'col', 'layer')), may hold values from 0 to 128, as said below
- exponents: float32 [5], replicated, may hold values from 0.02 to 1
Outputs:
- density_product: bfloat16 [2048, 16384], P('row', ('col', 'layer'))
- electron_density: float32 [256, 512, 512], P('row', 'col', 'layer')
The draws below stay inside these ranges and needn't reach their ends.
Inputs may be any that keep to these rules, and one draw needn't show every extreme that they name: `block_pattern`: symmetric, with ones on its diagonal; block_pattern[i, j] = 0 whenever |i - j| > 32 (no block couples to one more than 32 blocks away). `atom_functions`: all atoms' functions together are the 2048 rows of the window. `atom_offset`: row k of an atom lies in [0, the tile's cells along dimension k), that is 32, 32 or 128.
All inputs are finite; a program needn't handle non-finite values.
Results may differ from the reference program's by a relative error of at most 0.001.
Values may be sent and summed in bfloat16 or wider, within the bound.
A program may use at most 64 MiB of HBM per device.

```python
import math
import jax
import jax.numpy as jnp
import numpy as np
from jax import lax

BLK = 128
TX = 32
TY = 32
TZ = 128
HALO = 16
KINDS = 5
MOSTF = 9
NBASIS = 16384
ROWS = 2048
ATOMS = 512
SLOTS = 1
NX = 256
NY = 512
NZ = 512
N_ROW = 8
N_COL = 16
N_LAYER = 4


def draw_block_pattern(key, part):
    block_count = NBASIS // BLK
    reach_of = jax.random.randint(key, (block_count,), 1, max(2, block_count // 4) + 1)
    positions = jnp.arange(block_count, dtype=jnp.int32)
    separation = jnp.abs(positions[:, None] - positions[None, :])
    limit_of = jnp.maximum(reach_of[:, None], reach_of[None, :])
    return (separation <= limit_of).astype(jnp.int32)


def draw_atom_offset(key, part):
    uniform_draw = jax.random.uniform(key, (3, ATOMS), jnp.float32)
    spread = 0.001 + 0.998 * uniform_draw
    extent = jnp.array([TX, TY, TZ], jnp.float32)
    return spread * extent[:, None]


def place_ends(drawn, stream_key, low, largest):
    dims = drawn.shape
    index_at = [jax.random.randint(jax.random.fold_in(stream_key, axis), (), 0, dims[axis]) for axis in range(len(dims))]
    drawn = drawn.at[tuple(index_at)].set(low)
    longest = dims.index(max(dims))
    index_at[longest] = (index_at[longest] + 1) % dims[longest]
    return drawn.at[tuple(index_at)].set(largest)


def block_scale(stream_key, shape, split, least, largest):
    loudness, own = 1.0, jax.random.fold_in(stream_key, 6)
    for position, parts in split:
        draws = jnp.exp(jax.random.uniform(jax.random.fold_in(own, position), (parts,), jnp.float32, least / len(split), largest / len(split)))
        loudness = loudness * jnp.repeat(draws, shape[position] // parts).reshape([-1 if axis == position else 1 for axis in range(len(shape))])
    return loudness


def length_profile(count, total, bound, skew):
    weights = [(1 << 20) // math.isqrt(rank ** skew) + 1 for rank in range(2, count + 1)]
    rest, counts = total - bound - (count - 1), [1] * (count - 1)
    while rest > 0:
        free = [i for i in range(count - 1) if counts[i] < bound]
        mass, remaining = sum([weights[i] for i in free]), rest
        for i in free:
            extra = min(bound - counts[i], max(1, remaining * weights[i] // mass), rest)
            counts[i] = counts[i] + extra
            rest = rest - extra
    return np.array([bound] + counts)


def uneven_parts(rng, count, total, bound, lean):
    if count == 2:
        one = jax.random.randint(rng, (), max(1, total - bound), min(bound, total - 1) + 1)
        return jnp.stack([one, total - one])
    sizes = jnp.asarray(length_profile(count, total, bound, lean), jnp.int32)
    twos = (count - 1) // 2
    giver, receiver = sizes[1:1 + 2 * twos:2], sizes[2:2 + 2 * twos:2]
    room = jnp.minimum(giver - 1, bound - receiver)
    moved = jax.random.randint(jax.random.fold_in(rng, 1), (twos,), 0, 1 << 20) % (room + 1)
    sizes = sizes.at[1:1 + 2 * twos:2].set(giver - moved).at[2:2 + 2 * twos:2].set(receiver + moved)
    return sizes[jax.random.permutation(jax.random.fold_in(rng, 2), count)]


def noise(key, dims, width, limit, shards=(), kind=jnp.bfloat16):
    values = jax.random.normal(key, dims, jnp.float32) * width
    if len(shards) > 0:
        values = block_scale(key, dims, shards, -0.22, 0.18) * values
    return jnp.clip(values, min=-limit, max=limit).astype(kind)


def setup_inputs(seed: int = 0) -> dict:
    keys = jax.random.split(jax.random.key(seed), 8)
    density = noise(keys[0], (ROWS, NBASIS), 1.0, 6.0, ((0, 8), (1, 64)))
    margin = noise(keys[1], (NBASIS, NBASIS), (NBASIS // 4) ** -0.5, 0.09375, ((0, 32), (1, 16)))
    block_pattern = draw_block_pattern(jax.random.fold_in(keys[7], 71), 0)
    atom_functions = uneven_parts(keys[3], ATOMS, ROWS, MOSTF, 1).astype(jnp.int32)
    atom_kind = place_ends(jax.random.randint(keys[4], (ATOMS,), 0, KINDS), jax.random.fold_in(keys[4], 1), 0, KINDS - 1).astype(jnp.int32)
    atom_offset = draw_atom_offset(jax.random.fold_in(keys[7], 71), 0)
    exponents = jnp.clip(jnp.exp(jax.random.uniform(keys[6], (KINDS,), jnp.float32, math.log(0.02), math.log(1.0))), 0.02, 1.0)
    return {"density": density, "margin": margin, "block_pattern": block_pattern, "atom_functions": atom_functions, "atom_kind": atom_kind, "atom_offset": atom_offset, "exponents": exponents}


def block_masked(matrix, pattern):
    row_blocks = matrix.shape[0] // BLK
    col_blocks = matrix.shape[1] // BLK
    shaped = matrix.reshape(row_blocks, BLK, col_blocks, BLK)
    gate_mask = pattern[:row_blocks, :col_blocks].astype(jnp.bfloat16)
    return (shaped * gate_mask[:, None, :, None]).reshape(matrix.shape)


def axis_profile(anchor, offset, exponent_of, extent):
    cell_index = jnp.arange(extent, dtype=jnp.int32)
    relative = cell_index[None, :] - anchor[:, None]
    relative = (relative + HALO) % extent - HALO
    distance = relative.astype(jnp.float32) - offset[:, None]
    return jnp.where(jnp.abs(distance) <= HALO, jnp.exp(-exponent_of[:, None] * distance * distance), 0.0)


def reference(density, margin, block_pattern, atom_functions, atom_kind, atom_offset, exponents):
    masked_density = block_masked(density, block_pattern)
    masked_margin = block_masked(margin, block_pattern)
    product = jnp.dot(masked_density, masked_margin, preferred_element_type=jnp.float32)
    diagonal = jnp.diagonal(product[:, :ROWS])
    run_ends = jnp.cumsum(atom_functions, dtype=jnp.int32)
    owners = jnp.searchsorted(run_ends, jnp.arange(ROWS, dtype=jnp.int32), side="right")
    populations = jax.ops.segment_sum(diagonal, owners, num_segments=ATOMS)
    atom_ids = jnp.arange(ATOMS, dtype=jnp.int32)
    tile_of = atom_ids // SLOTS
    anchor_x = (tile_of // (N_COL * N_LAYER)) * TX
    anchor_y = ((tile_of // N_LAYER) % N_COL) * TY
    anchor_z = (tile_of % N_LAYER) * TZ
    exponent_of = exponents[atom_kind]
    weight_x = populations[:, None] * axis_profile(anchor_x, atom_offset[0], exponent_of, NX)
    along_y = axis_profile(anchor_y, atom_offset[1], exponent_of, NY)
    along_z = axis_profile(anchor_z, atom_offset[2], exponent_of, NZ)

    def slab(first_cell):
        part_x = lax.dynamic_slice_in_dim(weight_x, first_cell, TX, 1)
        paired = part_x[:, :, None] * along_y[:, None, :]
        return jnp.einsum("axy,az->xyz", paired, along_z, precision=lax.Precision.HIGHEST)

    slabs = lax.map(slab, jnp.arange(N_ROW, dtype=jnp.int32) * TX)
    return product.astype(jnp.bfloat16), slabs.reshape(NX, NY, NZ)
```

```python
import jax
import jax.numpy as jnp
from jax import lax
from jax.experimental import pallas as pl
from jax.experimental.pallas import tpu as pltpu
from jax.sharding import PartitionSpec as P

BLK = 128
TX = 32
TY = 32
TZ = 128
HALO = 16

MESH = pl.DeviceIdType.MESH


def spread_kernel(part_ref, out_ref, mine, slots, send_a, recv_a, send_b, recv_b):
    row = lax.axis_index("row")
    col = lax.axis_index("col")
    layer = lax.axis_index("layer")
    n_row = slots.shape[0]
    n_layer = lax.axis_size("layer")
    others = lax.axis_size("col") * n_layer
    home_col = row // n_layer
    home_layer = row % n_layer
    home = (col == home_col) & (layer == home_layer)
    barrier = pltpu.get_barrier_semaphore()

    @pl.when(jnp.logical_not(home))
    def _():
        pl.semaphore_signal(
            barrier, inc=1, device_id=(row, home_col, home_layer), device_id_type=MESH
        )

    for step in range(1, n_row):
        mate = (row + step) % n_row
        pl.semaphore_signal(barrier, inc=1, device_id=(mate, col, layer), device_id_type=MESH)

    def copy_a(index):
        return pltpu.make_async_remote_copy(
            src_ref=part_ref,
            dst_ref=mine,
            send_sem=send_a.at[index],
            recv_sem=recv_a,
            device_id=(row, index // n_layer, index % n_layer),
            device_id_type=MESH,
        )

    def copies_b(source):
        return [
            pltpu.make_async_remote_copy(
                src_ref=source,
                dst_ref=slots.at[row],
                send_sem=send_b.at[step],
                recv_sem=recv_b.at[row],
                device_id=((row + step) % n_row, col, layer),
                device_id_type=MESH,
            )
            for step in range(1, n_row)
        ]

    @pl.when(home)
    def _():
        pl.semaphore_wait(barrier, others - 1 + n_row - 1)
        for copy in copies_b(part_ref):
            copy.start()
        own = col * n_layer + layer

        def send_one(step, carry):
            copy_a((own + step) % others).start()
            return carry

        def end_one(step, carry):
            copy_a((own + step) % others).wait_send()
            return carry

        lax.fori_loop(1, others, send_one, 0)
        lax.fori_loop(1, others, end_one, 0)
        for copy in copies_b(part_ref):
            copy.wait_send()

    @pl.when(jnp.logical_not(home))
    def _():
        pl.semaphore_wait(barrier, n_row - 1)
        copy_a(0).wait_recv()
        for copy in copies_b(mine):
            copy.start()
        for copy in copies_b(mine):
            copy.wait_send()

    for step in range(1, n_row):
        mate = (row + step) % n_row
        pltpu.make_async_remote_copy(
            src_ref=part_ref,
            dst_ref=slots.at[mate],
            send_sem=send_b.at[0],
            recv_sem=recv_b.at[mate],
            device_id=(mate, col, layer),
            device_id_type=MESH,
        ).wait_recv()

    @pl.when(home)
    def _():
        out_ref[...] = part_ref[...]

    @pl.when(jnp.logical_not(home))
    def _():
        out_ref[...] = mine[...]

    for step in range(1, n_row):
        out_ref[...] += slots[(row + step) % n_row]


def spread(part):
    n_row = lax.axis_size("row")
    others = lax.axis_size("col") * lax.axis_size("layer")
    return pl.pallas_call(
        spread_kernel,
        out_shape=jax.ShapeDtypeStruct(part.shape, part.dtype),
        in_specs=[pl.BlockSpec(memory_space=pltpu.VMEM)],
        out_specs=pl.BlockSpec(memory_space=pltpu.VMEM),
        scratch_shapes=[
            pltpu.VMEM(part.shape, part.dtype),
            pltpu.VMEM((n_row,) + part.shape, part.dtype),
            pltpu.SemaphoreType.DMA((others,)),
            pltpu.SemaphoreType.DMA,
            pltpu.SemaphoreType.DMA((n_row,)),
            pltpu.SemaphoreType.DMA((n_row,)),
        ],
        compiler_params=pltpu.CompilerParams(collective_id=0, has_side_effects=True),
    )(part)


def with_neighbours(block, axis):
    count = lax.axis_size(axis)
    upward = [(i, (i + 1) % count) for i in range(count)]
    downward = [(target, source) for source, target in upward]
    below = lax.ppermute(block, axis, upward)
    above = lax.ppermute(block, axis, downward)
    return jnp.concatenate([below, block, above], axis=0)


def near_profile(cells, tile_of, extent, offset, exponent_of):
    local = jnp.arange(cells, dtype=jnp.int32)[None, :] - tile_of[:, None] * extent
    distance = local.astype(jnp.float32) - offset[:, None]
    return jnp.where(
        jnp.abs(distance) <= HALO, jnp.exp(-exponent_of[:, None] * distance * distance), 0.0
    )


def collocate(near, weights):
    index = jnp.arange(27, dtype=jnp.int32)
    exponent_of = near[:, 0]
    along_x = near_profile(TX, index % 3 - 1, TX, near[:, 1], exponent_of)
    along_y = near_profile(TY, index // 3 % 3 - 1, TY, near[:, 2], exponent_of)
    along_z = near_profile(TZ, index // 9 - 1, TZ, near[:, 3], exponent_of)
    paired = (weights[:, None] * along_x)[:, :, None] * along_y[:, None, :]
    return jnp.einsum("axy,az->xyz", paired, along_z, precision=lax.Precision.HIGHEST)


def shards(density, margin, block_pattern, atom_functions, atom_kind, atom_offset, exponents):
    rows_here, piece_width = density.shape
    share_rows, share_cols = margin.shape
    n_row = lax.axis_size("row")
    n_col = lax.axis_size("col")
    n_layer = lax.axis_size("layer")
    row_index = lax.axis_index("row")
    col_index = lax.axis_index("col")
    layer_index = lax.axis_index("layer")
    exponent_here = kind_exponent(atom_kind, exponents)
    near = jnp.concatenate([exponent_here[:, None], atom_offset.T], axis=1)
    for axis in ("row", "col", "layer"):
        near = with_neighbours(near, axis)
    density_mask = lax.dynamic_slice(
        block_pattern,
        (row_index * (rows_here // BLK), (layer_index * n_col + col_index) * piece_width // BLK),
        (rows_here // BLK, piece_width // BLK),
    )
    masked = apply_pattern(density, density_mask)
    margin_mask = lax.dynamic_slice(
        block_pattern,
        ((layer_index * n_row + row_index) * share_rows // BLK, col_index * share_cols // BLK),
        (share_rows // BLK, share_cols // BLK),
    )
    margin_masked = apply_pattern(margin, margin_mask)
    paired_rows = margin_masked.reshape(share_rows // (2 * BLK), 2, BLK, share_cols)
    lend = [(0, 2), (1, 3)]
    lender = layer_index < 2
    margin_lent = lax.ppermute(paired_rows[:, 1], "layer", lend)
    density_lent = lax.ppermute(masked[:, BLK:], "layer", lend)
    margin_half = jnp.where(lender, paired_rows[:, 0], margin_lent).reshape(-1, share_cols)
    density_half = jnp.where(lender, masked[:, :BLK], density_lent)
    density_all = lax.all_gather(density_half, "col", axis=1, tiled=True)
    margin_all = lax.all_gather(margin_half, "row", axis=0, tiled=True)
    product_acc = jnp.dot(density_all, margin_all, preferred_element_type=jnp.float32)
    product = lax.psum_scatter(product_acc, "layer", scatter_dimension=1, tiled=True)
    strip_width = product.shape[1]
    rows_global = row_index * rows_here + jnp.arange(rows_here, dtype=jnp.int32)
    cols_global = (col_index * n_layer + layer_index) * strip_width + jnp.arange(
        strip_width, dtype=jnp.int32
    )
    on_diagonal = rows_global[:, None] == cols_global[None, :]
    diagonal_part = jnp.sum(jnp.where(on_diagonal, product, 0.0), axis=0)
    run_ends = jnp.cumsum(atom_functions, dtype=jnp.int32)
    run_starts = run_ends - atom_functions
    member = (cols_global[:, None] >= run_starts[None, :]) & (
        cols_global[:, None] < run_ends[None, :]
    )
    partial_pop = jnp.sum(jnp.where(member, diagonal_part[:, None], 0.0), axis=0)
    all_pop = spread(partial_pop.reshape(-1, 128)).reshape(-1)
    index = jnp.arange(27, dtype=jnp.int32)
    near_atom = (
        ((row_index + index % 3 - 1) % n_row) * n_col + (col_index + index // 3 % 3 - 1) % n_col
    ) * n_layer + (layer_index + index // 9 - 1) % n_layer
    atoms = jnp.arange(all_pop.shape[0], dtype=jnp.int32)
    weights = jnp.sum(jnp.where(near_atom[:, None] == atoms[None, :], all_pop[None, :], 0.0), axis=1)
    return (product.astype(jnp.bfloat16), collocate(near, weights))


def apply_pattern(matrix, pattern_part):
    row_blocks = matrix.shape[0] // BLK
    col_blocks = matrix.shape[1] // BLK
    shaped = matrix.reshape(row_blocks, BLK, col_blocks, BLK)
    gate_mask = pattern_part.astype(jnp.bfloat16)
    return (shaped * gate_mask[:, None, :, None]).reshape(matrix.shape)


def kind_exponent(kinds_of, exponents):
    kind_match = kinds_of[:, None] == jnp.arange(exponents.shape[0], dtype=jnp.int32)[None, :]
    return jnp.sum(jnp.where(kind_match, exponents[None, :], 0.0), axis=1)


def solution(mesh):
    placed = (
        P("row", ("layer", "col")),
        P(("layer", "row"), "col"),
        P(),
        P(),
        P(("row", "col", "layer")),
        P(None, ("row", "col", "layer")),
        P(),
    )
    return jax.shard_map(
        shards,
        mesh=mesh,
        in_specs=placed,
        out_specs=(P("row", ("col", "layer")), P("row", "col", "layer")),
        check_vma=False,
    )
```

```python
import jax
import jax.numpy as jnp
from jax import lax
from jax.experimental import pallas as pl
from jax.experimental.pallas import tpu as pltpu
from jax.sharding import PartitionSpec as P

BLK = 128
TX = 32
TY = 32
TZ = 128
HALO = 16

MESH = pl.DeviceIdType.MESH


def spread_kernel(part_ref, out_ref, mine, slots, send_a, recv_a, send_b, recv_b):
    row = lax.axis_index("row")
    col = lax.axis_index("col")
    layer = lax.axis_index("layer")
    n_row = slots.shape[0]
    n_layer = lax.axis_size("layer")
    others = lax.axis_size("col") * n_layer
    home_col = row // n_layer
    home_layer = row % n_layer
    home = (col == home_col) & (layer == home_layer)
    barrier = pltpu.get_barrier_semaphore()

    @pl.when(jnp.logical_not(home))
    def _():
        pl.semaphore_signal(
            barrier, inc=1, device_id=(row, home_col, home_layer), device_id_type=MESH
        )

    for step in range(1, n_row):
        mate = (row + step) % n_row
        pl.semaphore_signal(barrier, inc=1, device_id=(mate, col, layer), device_id_type=MESH)

    def copy_a(index):
        return pltpu.make_async_remote_copy(
            src_ref=part_ref,
            dst_ref=mine,
            send_sem=send_a.at[index],
            recv_sem=recv_a,
            device_id=(row, index // n_layer, index % n_layer),
            device_id_type=MESH,
        )

    def copies_b(source):
        return [
            pltpu.make_async_remote_copy(
                src_ref=source,
                dst_ref=slots.at[row],
                send_sem=send_b.at[step],
                recv_sem=recv_b.at[row],
                device_id=((row + step) % n_row, col, layer),
                device_id_type=MESH,
            )
            for step in range(1, n_row)
        ]

    @pl.when(home)
    def _():
        pl.semaphore_wait(barrier, others - 1 + n_row - 1)
        for copy in copies_b(part_ref):
            copy.start()
        own = col * n_layer + layer

        def send_one(step, carry):
            copy_a((own + step) % others).start()
            return carry

        def end_one(step, carry):
            copy_a((own + step) % others).wait_send()
            return carry

        lax.fori_loop(1, others, send_one, 0)
        lax.fori_loop(1, others, end_one, 0)
        for copy in copies_b(part_ref):
            copy.wait_send()

    @pl.when(jnp.logical_not(home))
    def _():
        pl.semaphore_wait(barrier, n_row - 1)
        copy_a(0).wait_recv()
        for copy in copies_b(mine):
            copy.start()
        for copy in copies_b(mine):
            copy.wait_send()

    for step in range(1, n_row):
        mate = (row + step) % n_row
        pltpu.make_async_remote_copy(
            src_ref=part_ref,
            dst_ref=slots.at[mate],
            send_sem=send_b.at[0],
            recv_sem=recv_b.at[mate],
            device_id=(mate, col, layer),
            device_id_type=MESH,
        ).wait_recv()

    @pl.when(home)
    def _():
        out_ref[...] = part_ref[...]

    @pl.when(jnp.logical_not(home))
    def _():
        out_ref[...] = mine[...]

    for step in range(1, n_row):
        out_ref[...] += slots[(row + step) % n_row]


def spread(part):
    n_row = lax.axis_size("row")
    others = lax.axis_size("col") * lax.axis_size("layer")
    return pl.pallas_call(
        spread_kernel,
        out_shape=jax.ShapeDtypeStruct(part.shape, part.dtype),
        in_specs=[pl.BlockSpec(memory_space=pltpu.VMEM)],
        out_specs=pl.BlockSpec(memory_space=pltpu.VMEM),
        scratch_shapes=[
            pltpu.VMEM(part.shape, part.dtype),
            pltpu.VMEM((n_row,) + part.shape, part.dtype),
            pltpu.SemaphoreType.DMA((others,)),
            pltpu.SemaphoreType.DMA,
            pltpu.SemaphoreType.DMA((n_row,)),
            pltpu.SemaphoreType.DMA((n_row,)),
        ],
        compiler_params=pltpu.CompilerParams(collective_id=0, has_side_effects=True),
    )(part)


REACH = 32


def wanted_cols(window_blocks, col_blocks):
    return (window_blocks + 2 * REACH + col_blocks - 1) // col_blocks


def gather_kernel(
    density_ref, margin_ref, near_ref, product_ref, near_out,
    dens, marg, around,
    sem_around, got_around, sem_piece, sem_ring, sem_pair, got_slab, got_pair,
    sem_strip, sem_y, sem_half, got_strip, got_half,
):
    row = lax.axis_index("row")
    col = lax.axis_index("col")
    layer = lax.axis_index("layer")
    n_row = lax.axis_size("row")
    n_col = lax.axis_size("col")
    n_layer = lax.axis_size("layer")
    share, strip = marg.shape[1], marg.shape[2]
    slab = dens.shape[1] // 2
    y, x = row // 2, row % 2
    part = layer % 2
    live = col < wanted_cols(n_row * dens.shape[1] // BLK, margin_ref.shape[1] // BLK)
    rows_of = (n_row, marg.shape[0] - n_row)
    cols_of = (n_col, dens.shape[0] - n_col)

    def remote(source, target, sent, got, device):
        return pltpu.make_async_remote_copy(
            src_ref=source, dst_ref=target, send_sem=sent, recv_sem=got,
            device_id=device, device_id_type=MESH,
        )

    def when(condition, body):
        pl.when(condition)(body)

    shifts = [
        (dr, dc, dl) for dl in (-1, 0, 1) for dc in (-1, 0, 1) for dr in (-1, 0, 1)
    ]
    plane = [(xx, ll) for ll in range(n_layer) for xx in range(2)]
    up, down = ((row + 2) % n_row, col, layer), ((row + n_row - 2) % n_row, col, layer)
    onward, back = (row, (col + 1) % n_col, layer), (row, (col + n_col - 1) % n_col, layer)
    partner = (row, col, layer + 1 - 2 * part)

    def shifted(shift):
        return (
            (row + shift[0] + n_row) % n_row,
            (col + shift[1] + n_col) % n_col,
            (layer + shift[2] + n_layer) % n_layer,
        )

    barrier = pltpu.get_barrier_semaphore()
    for shift in shifts:
        if shift != (0, 0, 0):
            pl.semaphore_signal(barrier, inc=1, device_id=shifted(shift), device_id_type=MESH)
    for device in (up, down):
        pl.semaphore_signal(barrier, inc=1, device_id=device, device_id_type=MESH)
    for xx in range(2):
        for step in range(n_layer):
            if (xx, step) != (0, 0):
                device = (2 * y + (x + xx) % 2, col, (layer + step) % n_layer)
                pl.semaphore_signal(barrier, inc=1, device_id=device, device_id_type=MESH)
    pl.semaphore_wait(barrier, 26 + 2 + 7)

    def piece_copy(kind, target_layer, start):
        slot = dens.at[kind * n_col + col, pl.ds(slab * (target_layer % 2), slab)]
        source = density_ref.at[pl.ds(slab * (target_layer % 2), slab)]
        sent, got = sem_piece.at[target_layer], got_slab.at[kind * n_col + col]
        here = layer == target_layer
        far = remote(source, slot, sent, got, (row, col, target_layer))
        if start:
            when(here, pltpu.make_async_copy(source, slot, got).start)
        when(jnp.logical_not(here), far.start if start else far.wait_send)

    def strip_copy(kind, target, start):
        xx, ll = target
        slot = marg.at[kind * n_row + row]
        source = margin_ref.at[:, pl.ds(strip * ll, strip)]
        sent, got = sem_strip.at[ll * 2 + xx], got_strip.at[kind * n_row + row]
        here = (layer == ll) & (x == xx)
        far = remote(source, slot, sent, got, (2 * y + xx, col, ll))
        if start:
            when(here, pltpu.make_async_copy(source, slot, got).start)
        when(jnp.logical_not(here), far.start if start else far.wait_send)

    def first_copies(start):
        for kind in range(2):

            def pieces(kind=kind):
                for ll in range(n_layer):
                    piece_copy(kind, ll, start)

            def strips(kind=kind):
                for target in plane:
                    strip_copy(kind, target, start)

            when((layer == kind) & (col < cols_of[kind]), pieces)
            when((layer == kind) & (row < rows_of[kind]) & live, strips)

    def around_copy(index):
        dr, dc, dl = shifts[index]
        return remote(
            near_ref, around.at[26 - index], sem_around.at[index], got_around.at[26 - index],
            shifted(shifts[index]),
        )

    def slab_of(kind, origin, half):
        return dens.at[kind * n_col + origin, pl.ds(pl.multiple_of(slab * half, slab), slab)]

    def ring_copy(kind, origin, way, step):
        block = slab_of(kind, origin, part)
        return remote(
            block, block, sem_ring.at[kind, way, step], got_slab.at[kind * n_col + origin],
            (onward, back)[way],
        )

    def pair_copy(kind, origin):
        block = slab_of(kind, origin, part)
        return remote(
            block, block, sem_pair.at[kind * n_col + origin],
            got_pair.at[kind * n_col + origin], partner,
        )

    def pair_wait(kind, origin):
        block = slab_of(kind, origin, 1 - part)
        remote(
            block, block, sem_pair.at[kind * n_col + origin],
            got_pair.at[kind * n_col + origin], partner,
        ).wait_recv()

    def ring_step(step, start):
        half = n_col // 2
        for way in ((0, 1) if step and step < half else (0,)):
            origin = (col + (n_col - step if way == 0 else step)) % n_col
            for kind in range(2):

                def body(kind=kind, origin=origin, way=way):
                    if start:
                        ring_copy(kind, origin, way, 0).wait_recv()
                    sends = [pair_copy(kind, origin)]
                    if way == 0 and step < half:
                        sends.append(ring_copy(kind, origin, 0, step))
                    if step == 0 or (way == 1 and step < half - 1):
                        sends.append(ring_copy(kind, origin, 1, step))
                    for copy in reversed(sends):
                        if start:
                            copy.start()
                        else:
                            copy.wait_send()

                when(origin < cols_of[kind], body)

    def own_strip(kind, other, start):
        origin = 2 * y + (x + other) % 2
        block = marg.at[kind * n_row + origin]
        got = got_strip.at[kind * n_row + origin]

        def body():
            copies = [
                remote(block, block, sem_y.at[kind, other, way], got, (up, down)[way])
                for way in range(2)
            ]
            if start:
                copies[0].wait_recv()
            for copy in copies:
                if start:
                    copy.start()
                else:
                    copy.wait_send()

        when(live & (origin < rows_of[kind]), body)

    def next_strip(kind, xx, way, start):
        origin = 2 * ((y + (3 if way == 0 else 1)) % 4) + xx
        whole = marg.at[kind * n_row + origin]
        block = marg.at[kind * n_row + origin, pl.ds(share // 2 * way, share // 2)]

        def body():
            if start:
                remote(
                    whole, whole, sem_y.at[kind, xx, way], got_strip.at[kind * n_row + origin], up
                ).wait_recv()
            copy = remote(
                block, block, sem_half.at[kind, xx, way],
                got_half.at[kind * n_row + origin, way], (up, down)[way],
            )
            if start:
                copy.start()
            else:
                copy.wait_send()

        when(live & (origin < rows_of[kind]), body)

    def far_strip(kind, xx):
        origin = 2 * ((y + 2) % 4) + xx

        def body():
            for way in range(2):
                block = marg.at[kind * n_row + origin, pl.ds(share // 2 * way, share // 2)]
                remote(
                    block, block, sem_half.at[kind, xx, way],
                    got_half.at[kind * n_row + origin, way], up,
                ).wait_recv()

        when(live & (origin < rows_of[kind]), body)

    def relays(start):
        ring_step(0, start)
        own_strip(0, 0, start)
        ring_step(1, start)
        own_strip(1, 0, start)
        ring_step(2, start)
        ring_step(3, start)
        own_strip(0, 1, start)
        ring_step(4, start)
        ring_step(5, start)
        own_strip(1, 1, start)
        ring_step(6, start)
        for way in range(2):
            for xx in range(2):
                next_strip(0, xx, way, start)
        ring_step(7, start)
        for way in range(2):
            for xx in range(2):
                next_strip(1, xx, way, start)
        ring_step(8, start)

    first_copies(True)
    for index in range(27):
        if index != 13:
            around_copy(index).start()
    relays(True)
    for kind in range(2):
        for origin in range(cols_of[kind]):
            pair_wait(kind, origin)
        for xx in range(2):
            far_strip(kind, xx)

    @pl.when(live)
    def _():
        product_ref[...] = jnp.zeros_like(product_ref)

        def add_share(j, carry):
            for side in range(2):
                product_ref[...] += jnp.dot(
                    dens[2 * j + side],
                    marg[j, pl.ds(share // 2 * side, share // 2)],
                    preferred_element_type=jnp.float32,
                )
            return carry

        lax.fori_loop(0, marg.shape[0], add_share, 0)

    @pl.when(jnp.logical_not(live))
    def _():
        product_ref[...] = jnp.zeros_like(product_ref)

    for index in range(27):
        if index != 13:
            around_copy(26 - index).wait_recv()
            near_out[index] = around[index]
    near_out[13] = near_ref[...]
    first_copies(False)
    for index in range(27):
        if index != 13:
            around_copy(index).wait_send()
    relays(False)


def gather_product(density, margin, near):
    rows_here, piece_width = density.shape
    share, share_cols = margin.shape
    n_row, n_col, n_layer = (lax.axis_size(axis) for axis in ("row", "col", "layer"))
    depth = n_row * rows_here + REACH * BLK
    strip = share_cols // n_layer
    dma = pltpu.SemaphoreType.DMA
    vmem = pl.BlockSpec(memory_space=pltpu.VMEM)
    anywhere = pl.BlockSpec(memory_space=pl.ANY)
    pieces, shares = depth // piece_width, depth // share
    return pl.pallas_call(
        gather_kernel,
        out_shape=(
            jax.ShapeDtypeStruct((rows_here, strip), jnp.float32),
            jax.ShapeDtypeStruct((27,) + near.shape, jnp.float32),
        ),
        in_specs=[anywhere, anywhere, vmem],
        out_specs=(vmem, vmem),
        scratch_shapes=[
            pltpu.VMEM((pieces, rows_here, piece_width), jnp.bfloat16),
            pltpu.VMEM((shares, share, strip), jnp.bfloat16),
            pltpu.VMEM((27,) + near.shape, jnp.float32),
            dma((27,)),
            dma((27,)),
            dma((n_layer,)),
            dma((2, 2, n_col // 2)),
            dma((pieces,)),
            dma((pieces,)),
            dma((pieces,)),
            dma((2 * n_layer,)),
            dma((2, 2, 2)),
            dma((2, 2, 2)),
            dma((shares,)),
            dma((shares, 2)),
        ],
        compiler_params=pltpu.CompilerParams(
            collective_id=1, has_side_effects=True, vmem_limit_bytes=24 * 1024 * 1024
        ),
    )(density, margin, near)


def near_profile(cells, tile_of, extent, offset, exponent_of):
    local = jnp.arange(cells, dtype=jnp.int32)[None, :] - tile_of[:, None] * extent
    distance = local.astype(jnp.float32) - offset[:, None]
    return jnp.where(
        jnp.abs(distance) <= HALO, jnp.exp(-exponent_of[:, None] * distance * distance), 0.0
    )


def collocate(near, weights):
    index = jnp.arange(27, dtype=jnp.int32)
    exponent_of = near[:, 0]
    along_x = near_profile(TX, index % 3 - 1, TX, near[:, 1], exponent_of)
    along_y = near_profile(TY, index // 3 % 3 - 1, TY, near[:, 2], exponent_of)
    along_z = near_profile(TZ, index // 9 - 1, TZ, near[:, 3], exponent_of)
    paired = (weights[:, None] * along_x)[:, :, None] * along_y[:, None, :]
    return jnp.einsum("axy,az->xyz", paired, along_z, precision=lax.Precision.HIGHEST)


def shards(density, margin, block_pattern, atom_functions, atom_kind, atom_offset, exponents):
    rows_here, piece_width = density.shape
    share_rows, share_cols = margin.shape
    n_row = lax.axis_size("row")
    n_col = lax.axis_size("col")
    n_layer = lax.axis_size("layer")
    row_index = lax.axis_index("row")
    col_index = lax.axis_index("col")
    layer_index = lax.axis_index("layer")
    exponent_here = kind_exponent(atom_kind, exponents)
    near_here = jnp.concatenate([exponent_here[:, None], atom_offset.T], axis=1)
    near_here = jnp.broadcast_to(jnp.pad(near_here, ((0, 0), (0, 124))), (8, 128))
    density_mask = lax.dynamic_slice(
        block_pattern,
        (row_index * (rows_here // BLK), (layer_index * n_col + col_index) * piece_width // BLK),
        (rows_here // BLK, piece_width // BLK),
    )
    masked = apply_pattern(density, density_mask)
    margin_mask = lax.dynamic_slice(
        block_pattern,
        ((layer_index * n_row + row_index) * share_rows // BLK, col_index * share_cols // BLK),
        (share_rows // BLK, share_cols // BLK),
    )
    margin_masked = apply_pattern(margin, margin_mask)
    product, near_all = gather_product(masked, margin_masked, near_here)
    near = near_all[:, 0, :4]
    strip_width = product.shape[1]
    rows_global = row_index * rows_here + jnp.arange(rows_here, dtype=jnp.int32)
    cols_global = (col_index * n_layer + layer_index) * strip_width + jnp.arange(
        strip_width, dtype=jnp.int32
    )
    on_diagonal = rows_global[:, None] == cols_global[None, :]
    diagonal_part = jnp.sum(jnp.where(on_diagonal, product, 0.0), axis=0)
    run_ends = jnp.cumsum(atom_functions, dtype=jnp.int32)
    run_starts = run_ends - atom_functions
    member = (cols_global[:, None] >= run_starts[None, :]) & (
        cols_global[:, None] < run_ends[None, :]
    )
    partial_pop = jnp.sum(jnp.where(member, diagonal_part[:, None], 0.0), axis=0)
    all_pop = spread(partial_pop.reshape(-1, 128)).reshape(-1)
    index = jnp.arange(27, dtype=jnp.int32)
    near_atom = (
        ((row_index + index % 3 - 1) % n_row) * n_col + (col_index + index // 3 % 3 - 1) % n_col
    ) * n_layer + (layer_index + index // 9 - 1) % n_layer
    atoms = jnp.arange(all_pop.shape[0], dtype=jnp.int32)
    weights = jnp.sum(jnp.where(near_atom[:, None] == atoms[None, :], all_pop[None, :], 0.0), axis=1)
    return (product.astype(jnp.bfloat16), collocate(near, weights))


def apply_pattern(matrix, pattern_part):
    row_blocks = matrix.shape[0] // BLK
    col_blocks = matrix.shape[1] // BLK
    shaped = matrix.reshape(row_blocks, BLK, col_blocks, BLK)
    gate_mask = pattern_part.astype(jnp.bfloat16)
    return (shaped * gate_mask[:, None, :, None]).reshape(matrix.shape)


def kind_exponent(kinds_of, exponents):
    kind_match = kinds_of[:, None] == jnp.arange(exponents.shape[0], dtype=jnp.int32)[None, :]
    return jnp.sum(jnp.where(kind_match, exponents[None, :], 0.0), axis=1)


def solution(mesh):
    placed = (
        P("row", ("layer", "col")),
        P(("layer", "row"), "col"),
        P(),
        P(),
        P(("row", "col", "layer")),
        P(None, ("row", "col", "layer")),
        P(),
    )
    return jax.shard_map(
        shards,
        mesh=mesh,
        in_specs=placed,
        out_specs=(P("row", ("col", "layer")), P("row", "col", "layer")),
        check_vma=False,
    )
```

```python
import jax
import jax.numpy as jnp
from jax import lax
from jax.experimental import pallas as pl
from jax.experimental.pallas import tpu as pltpu
from jax.sharding import PartitionSpec as P

BLK = 128
TX = 32
TY = 32
TZ = 128
HALO = 16

MESH = pl.DeviceIdType.MESH


REACH = 32


def wanted_cols(window_blocks, col_blocks):
    return (window_blocks + 2 * REACH + col_blocks - 1) // col_blocks


def gather_kernel(
    density_ref, margin_ref, near_ref, bounds_ref, product_ref, near_out, pops_out,
    dens, marg, around, pops_home, pops_mine, pops_rows,
    sem_spread, got_mine, sem_rows, got_rows, sem_around, got_around, sem_piece, sem_ring, sem_pair, got_slab, got_pair,
    sem_strip, sem_y, sem_half, got_strip, got_half,
):
    row = lax.axis_index("row")
    col = lax.axis_index("col")
    layer = lax.axis_index("layer")
    n_row = lax.axis_size("row")
    n_col = lax.axis_size("col")
    n_layer = lax.axis_size("layer")
    share, strip = marg.shape[1], marg.shape[2]
    slab = dens.shape[1] // 2
    y, x = row // 2, row % 2
    part = layer % 2
    live = col < wanted_cols(n_row * dens.shape[1] // BLK, margin_ref.shape[1] // BLK)
    rows_of = (n_row, marg.shape[0] - n_row)
    cols_of = (n_col, dens.shape[0] - n_col)

    def remote(source, target, sent, got, device):
        return pltpu.make_async_remote_copy(
            src_ref=source, dst_ref=target, send_sem=sent, recv_sem=got,
            device_id=device, device_id_type=MESH,
        )

    def when(condition, body):
        pl.when(condition)(body)

    shifts = [
        (dr, dc, dl) for dl in (-1, 0, 1) for dc in (-1, 0, 1) for dr in (-1, 0, 1)
    ]
    plane = [(0, 2), (1, 2), (0, 3), (1, 3), (0, 0), (0, 1), (1, 0), (1, 1)]
    home_col, home_layer = row // n_layer, row % n_layer
    home = (col == home_col) & (layer == home_layer)
    members = n_col * n_layer
    up, down = ((row + 2) % n_row, col, layer), ((row + n_row - 2) % n_row, col, layer)
    onward, back = (row, (col + 1) % n_col, layer), (row, (col + n_col - 1) % n_col, layer)
    partner = (row, col, layer + 1 - 2 * part)

    def shifted(shift):
        return (
            (row + shift[0] + n_row) % n_row,
            (col + shift[1] + n_col) % n_col,
            (layer + shift[2] + n_layer) % n_layer,
        )

    barrier = pltpu.get_barrier_semaphore()
    for shift in shifts:
        if shift != (0, 0, 0):
            pl.semaphore_signal(barrier, inc=1, device_id=shifted(shift), device_id_type=MESH)
    for device in (up, down):
        pl.semaphore_signal(barrier, inc=1, device_id=device, device_id_type=MESH)
    for xx in range(2):
        for step in range(n_layer):
            if (xx, step) != (0, 0):
                device = (2 * y + (x + xx) % 2, col, (layer + step) % n_layer)
                pl.semaphore_signal(barrier, inc=1, device_id=device, device_id_type=MESH)
    for step in range(1, n_row):
        device = ((row + step) % n_row, col, layer)
        pl.semaphore_signal(barrier, inc=1, device_id=device, device_id_type=MESH)

    @pl.when(home)
    def _():
        pl.semaphore_wait(barrier, 26 + 2 + 7 + n_row - 1 + members - 1)

    @pl.when(jnp.logical_not(home))
    def _():
        device = (row, home_col, home_layer)
        pl.semaphore_signal(barrier, inc=1, device_id=device, device_id_type=MESH)
        pl.semaphore_wait(barrier, 26 + 2 + 7 + n_row - 1)

    def piece_copy(kind, target_layer, start):
        slot = dens.at[kind * n_col + col, pl.ds(slab * (target_layer % 2), slab)]
        source = density_ref.at[pl.ds(slab * (target_layer % 2), slab)]
        sent, got = sem_piece.at[target_layer], got_slab.at[kind * n_col + col]
        here = layer == target_layer
        far = remote(source, slot, sent, got, (row, col, target_layer))
        if start:
            when(here, pltpu.make_async_copy(source, slot, got).start)
        when(jnp.logical_not(here), far.start if start else far.wait_send)

    def strip_copy(kind, target, start):
        other, ll = target
        xx = (x + other) % 2
        slot = marg.at[kind * n_row + row]
        source = margin_ref.at[:, pl.ds(strip * ll, strip)]
        sent, got = sem_strip.at[ll * 2 + other], got_strip.at[kind * n_row + row]
        here = (layer == ll) & (other == 0)
        far = remote(source, slot, sent, got, (2 * y + xx, col, ll))
        if start and other == 0:
            when(here, pltpu.make_async_copy(source, slot, got).start)
        when(jnp.logical_not(here), far.start if start else far.wait_send)

    def first_copies(start):
        for kind in range(2):

            def pieces(kind=kind):
                for ll in (2, 3, 0, 1):
                    piece_copy(kind, ll, start)

            def strips(kind=kind):
                for target in plane:
                    strip_copy(kind, target, start)

            when((layer == kind) & (col < cols_of[kind]), pieces)
            when((layer == kind) & (row < rows_of[kind]) & live, strips)

    def around_copy(index):
        dr, dc, dl = shifts[index]
        return remote(
            near_ref, around.at[26 - index], sem_around.at[index], got_around.at[26 - index],
            shifted(shifts[index]),
        )

    def slab_of(kind, origin, half):
        return dens.at[kind * n_col + origin, pl.ds(pl.multiple_of(slab * half, slab), slab)]

    def ring_copy(kind, origin, way, step):
        block = slab_of(kind, origin, part)
        return remote(
            block, block, sem_ring.at[kind, way, step], got_slab.at[kind * n_col + origin],
            (onward, back)[way],
        )

    def pair_copy(kind, origin):
        block = slab_of(kind, origin, part)
        return remote(
            block, block, sem_pair.at[kind * n_col + origin],
            got_pair.at[kind * n_col + origin], partner,
        )

    def pair_wait(kind, origin):
        block = slab_of(kind, origin, 1 - part)
        remote(
            block, block, sem_pair.at[kind * n_col + origin],
            got_pair.at[kind * n_col + origin], partner,
        ).wait_recv()

    def ring_step(step, start):
        half = n_col // 2
        for way in ((0, 1) if step and step < half else (0,)):
            origin = (col + (n_col - step if way == 0 else step)) % n_col
            for kind in range(2):

                def body(kind=kind, origin=origin, way=way):
                    if start:
                        ring_copy(kind, origin, way, 0).wait_recv()
                    sends = [pair_copy(kind, origin)]
                    if way == 0 and step < half:
                        sends.append(ring_copy(kind, origin, 0, step))
                    if step == 0 or (way == 1 and step < half - 1):
                        sends.append(ring_copy(kind, origin, 1, step))
                    for copy in reversed(sends):
                        if start:
                            copy.start()
                        else:
                            copy.wait_send()

                when(origin < cols_of[kind], body)

    def own_strip(kind, other, start):
        origin = 2 * y + (x + other) % 2
        block = marg.at[kind * n_row + origin]
        got = got_strip.at[kind * n_row + origin]

        def body():
            copies = [
                remote(block, block, sem_y.at[kind, other, way], got, (up, down)[way])
                for way in range(2)
            ]
            if start:
                copies[0].wait_recv()
            for copy in copies:
                if start:
                    copy.start()
                else:
                    copy.wait_send()

        when(live & (origin < rows_of[kind]), body)

    def next_strip(kind, other, way, start):
        origin = 2 * ((y + (3 if way == 0 else 1)) % 4) + (x + other) % 2
        whole = marg.at[kind * n_row + origin]
        block = marg.at[kind * n_row + origin, pl.ds(share // 2 * way, share // 2)]

        def body():
            if start:
                remote(
                    whole, whole, sem_y.at[kind, other, way], got_strip.at[kind * n_row + origin], up
                ).wait_recv()
            copy = remote(
                block, block, sem_half.at[kind, other, way],
                got_half.at[kind * n_row + origin, way], (up, down)[way],
            )
            if start:
                copy.start()
            else:
                copy.wait_send()

        when(live & (origin < rows_of[kind]), body)

    def far_strip(kind, xx):
        origin = 2 * ((y + 2) % 4) + xx

        def body():
            for way in range(2):
                block = marg.at[kind * n_row + origin, pl.ds(share // 2 * way, share // 2)]
                remote(
                    block, block, sem_half.at[kind, xx, way],
                    got_half.at[kind * n_row + origin, way], up,
                ).wait_recv()

        when(live & (origin < rows_of[kind]), body)

    def nexts(kind, other, start):
        for way in range(2):
            next_strip(kind, other, way, start)

    def relays_low(start):
        ring_step(0, start)
        own_strip(0, 0, start)
        own_strip(1, 0, start)
        ring_step(1, start)
        ring_step(2, start)
        nexts(0, 0, start)
        ring_step(3, start)
        ring_step(4, start)
        nexts(1, 0, start)
        ring_step(5, start)
        ring_step(6, start)
        own_strip(0, 1, start)
        ring_step(7, start)
        ring_step(8, start)
        own_strip(1, 1, start)
        nexts(0, 1, start)
        nexts(1, 1, start)

    def relays_high(start):
        ring_step(0, start)
        ring_step(1, start)
        own_strip(0, 1, start)
        ring_step(2, start)
        own_strip(0, 0, start)
        ring_step(3, start)
        own_strip(1, 1, start)
        ring_step(4, start)
        own_strip(1, 0, start)
        ring_step(5, start)
        ring_step(6, start)
        nexts(0, 1, start)
        ring_step(7, start)
        nexts(0, 0, start)
        ring_step(8, start)
        nexts(1, 1, start)
        nexts(1, 0, start)

    def relays(start):
        when(layer < 2, lambda: relays_low(start))
        when(layer >= 2, lambda: relays_high(start))

    def spread_copy(index):
        return remote(
            pops_home, pops_mine, sem_spread.at[index], got_mine,
            (row, index // n_layer, index % n_layer),
        )

    def row_copies(source):
        return [
            remote(
                source, pops_rows.at[row], sem_rows.at[step], got_rows.at[row],
                ((row + step) % n_row, col, layer),
            )
            for step in range(1, n_row)
        ]

    def spread_step(start):
        def body(step, carry):
            copy = spread_copy((col * n_layer + layer + step) % members)
            if start:
                copy.start()
            else:
                copy.wait_send()
            return carry

        lax.fori_loop(1, members, body, 0)

    first_copies(True)
    for index in range(27):
        if index != 13:
            around_copy(index).start()
    relays(True)
    for kind in range(2):
        for origin in range(cols_of[kind]):
            pair_wait(kind, origin)
        for xx in range(2):
            far_strip(kind, xx)

    @pl.when(live)
    def _():
        product_ref[...] = jnp.zeros_like(product_ref)

        def add_share(j, carry):
            for side in range(2):
                product_ref[...] += jnp.dot(
                    dens[2 * j + side],
                    marg[j, pl.ds(share // 2 * side, share // 2)],
                    preferred_element_type=jnp.float32,
                )
            return carry

        lax.fori_loop(0, marg.shape[0], add_share, 0)

    @pl.when(jnp.logical_not(live))
    def _():
        product_ref[...] = jnp.zeros_like(product_ref)

    @pl.when(home)
    def _():
        side = product_ref.shape
        here = lax.broadcasted_iota(jnp.int32, side, 0) == lax.broadcasted_iota(jnp.int32, side, 1)
        diagonal = jnp.sum(jnp.where(here, product_ref[...], 0.0), axis=1, keepdims=True)
        wide = (side[0], bounds_ref.shape[1])
        function = lax.broadcasted_iota(jnp.int32, wide, 0) + row * side[0]
        member = (function >= bounds_ref[0:1, :]) & (function < bounds_ref[1:2, :])
        pops_home[...] = jnp.sum(jnp.where(member, diagonal, 0.0), axis=0, keepdims=True)

    for index in range(27):
        if index != 13:
            around_copy(26 - index).wait_recv()
            near_out[index] = around[index]
    near_out[13] = near_ref[...]

    @pl.when(home)
    def _():
        for copy in row_copies(pops_home):
            copy.start()
        spread_step(True)

    @pl.when(jnp.logical_not(home))
    def _():
        spread_copy(0).wait_recv()
        for copy in row_copies(pops_mine):
            copy.start()

    first_copies(False)
    for index in range(27):
        if index != 13:
            around_copy(index).wait_send()
    relays(False)
    for step in range(1, n_row):
        mate = (row + step) % n_row
        slot = pops_rows.at[mate]
        remote(slot, slot, sem_rows.at[0], got_rows.at[mate], (mate, col, layer)).wait_recv()

    @pl.when(home)
    def _():
        pops_out[...] = pops_home[...]
        spread_step(False)

    @pl.when(jnp.logical_not(home))
    def _():
        pops_out[...] = pops_mine[...]

    for step in range(1, n_row):
        pops_out[...] += pops_rows[(row + step) % n_row]
    for copy in row_copies(pops_mine):
        copy.wait_send()


def gather_product(density, margin, near, bounds):
    rows_here, piece_width = density.shape
    share, share_cols = margin.shape
    n_row, n_col, n_layer = (lax.axis_size(axis) for axis in ("row", "col", "layer"))
    depth = n_row * rows_here + REACH * BLK
    strip = share_cols // n_layer
    dma = pltpu.SemaphoreType.DMA
    vmem = pl.BlockSpec(memory_space=pltpu.VMEM)
    anywhere = pl.BlockSpec(memory_space=pl.ANY)
    pieces, shares = depth // piece_width, depth // share
    return pl.pallas_call(
        gather_kernel,
        out_shape=(
            jax.ShapeDtypeStruct((rows_here, strip), jnp.float32),
            jax.ShapeDtypeStruct((27,) + near.shape, jnp.float32),
            jax.ShapeDtypeStruct((1, bounds.shape[1]), jnp.float32),
        ),
        in_specs=[anywhere, anywhere, vmem, vmem],
        out_specs=(vmem, vmem, vmem),
        scratch_shapes=[
            pltpu.VMEM((pieces, rows_here, piece_width), jnp.bfloat16),
            pltpu.VMEM((shares, share, strip), jnp.bfloat16),
            pltpu.VMEM((27,) + near.shape, jnp.float32),
            pltpu.VMEM((1, bounds.shape[1]), jnp.float32),
            pltpu.VMEM((1, bounds.shape[1]), jnp.float32),
            pltpu.VMEM((n_row, 1, bounds.shape[1]), jnp.float32),
            dma((n_col * n_layer,)),
            dma,
            dma((n_row,)),
            dma((n_row,)),
            dma((27,)),
            dma((27,)),
            dma((n_layer,)),
            dma((2, 2, n_col // 2)),
            dma((pieces,)),
            dma((pieces,)),
            dma((pieces,)),
            dma((2 * n_layer,)),
            dma((2, 2, 2)),
            dma((2, 2, 2)),
            dma((shares,)),
            dma((shares, 2)),
        ],
        compiler_params=pltpu.CompilerParams(
            collective_id=1, has_side_effects=True, vmem_limit_bytes=24 * 1024 * 1024
        ),
    )(density, margin, near, bounds)


def near_profile(cells, tile_of, extent, offset, exponent_of):
    local = jnp.arange(cells, dtype=jnp.int32)[None, :] - tile_of[:, None] * extent
    distance = local.astype(jnp.float32) - offset[:, None]
    return jnp.where(
        jnp.abs(distance) <= HALO, jnp.exp(-exponent_of[:, None] * distance * distance), 0.0
    )


def collocate(near, weights):
    index = jnp.arange(27, dtype=jnp.int32)
    exponent_of = near[:, 0]
    along_x = near_profile(TX, index % 3 - 1, TX, near[:, 1], exponent_of)
    along_y = near_profile(TY, index // 3 % 3 - 1, TY, near[:, 2], exponent_of)
    along_z = near_profile(TZ, index // 9 - 1, TZ, near[:, 3], exponent_of)
    paired = (weights[:, None] * along_x)[:, :, None] * along_y[:, None, :]
    return jnp.einsum("axy,az->xyz", paired, along_z, precision=lax.Precision.HIGHEST)


def shards(density, margin, block_pattern, atom_functions, atom_kind, atom_offset, exponents):
    rows_here, piece_width = density.shape
    share_rows, share_cols = margin.shape
    n_row = lax.axis_size("row")
    n_col = lax.axis_size("col")
    n_layer = lax.axis_size("layer")
    row_index = lax.axis_index("row")
    col_index = lax.axis_index("col")
    layer_index = lax.axis_index("layer")
    exponent_here = kind_exponent(atom_kind, exponents)
    near_here = jnp.concatenate([exponent_here[:, None], atom_offset.T], axis=1)
    near_here = jnp.broadcast_to(jnp.pad(near_here, ((0, 0), (0, 124))), (8, 128))
    density_mask = lax.dynamic_slice(
        block_pattern,
        (row_index * (rows_here // BLK), (layer_index * n_col + col_index) * piece_width // BLK),
        (rows_here // BLK, piece_width // BLK),
    )
    masked = apply_pattern(density, density_mask)
    margin_mask = lax.dynamic_slice(
        block_pattern,
        ((layer_index * n_row + row_index) * share_rows // BLK, col_index * share_cols // BLK),
        (share_rows // BLK, share_cols // BLK),
    )
    margin_masked = apply_pattern(margin, margin_mask)
    run_ends = jnp.cumsum(atom_functions, dtype=jnp.int32)
    bounds = jnp.stack([run_ends - atom_functions, run_ends])
    product, near_all, pops = gather_product(masked, margin_masked, near_here, bounds)
    near = near_all[:, 0, :4]
    all_pop = pops.reshape(-1)
    index = jnp.arange(27, dtype=jnp.int32)
    near_atom = (
        ((row_index + index % 3 - 1) % n_row) * n_col + (col_index + index // 3 % 3 - 1) % n_col
    ) * n_layer + (layer_index + index // 9 - 1) % n_layer
    atoms = jnp.arange(all_pop.shape[0], dtype=jnp.int32)
    weights = jnp.sum(jnp.where(near_atom[:, None] == atoms[None, :], all_pop[None, :], 0.0), axis=1)
    return (product.astype(jnp.bfloat16), collocate(near, weights))


def apply_pattern(matrix, pattern_part):
    row_blocks = matrix.shape[0] // BLK
    col_blocks = matrix.shape[1] // BLK
    shaped = matrix.reshape(row_blocks, BLK, col_blocks, BLK)
    gate_mask = pattern_part.astype(jnp.bfloat16)
    return (shaped * gate_mask[:, None, :, None]).reshape(matrix.shape)


def kind_exponent(kinds_of, exponents):
    kind_match = kinds_of[:, None] == jnp.arange(exponents.shape[0], dtype=jnp.int32)[None, :]
    return jnp.sum(jnp.where(kind_match, exponents[None, :], 0.0), axis=1)


def solution(mesh):
    placed = (
        P("row", ("layer", "col")),
        P(("layer", "row"), "col"),
        P(),
        P(),
        P(("row", "col", "layer")),
        P(None, ("row", "col", "layer")),
        P(),
    )
    return jax.shard_map(
        shards,
        mesh=mesh,
        in_specs=placed,
        out_specs=(P("row", ("col", "layer")), P("row", "col", "layer")),
        check_vma=False,
    )
```

```python
import jax
import jax.numpy as jnp
from jax import lax
from jax.experimental import pallas as pl
from jax.experimental.pallas import tpu as pltpu
from jax.sharding import PartitionSpec as P

BLK = 128
TX = 32
TY = 32
TZ = 128
HALO = 16

MESH = pl.DeviceIdType.MESH


REACH = 32


def wanted_cols(window_blocks, col_blocks):
    return (window_blocks + 2 * REACH + col_blocks - 1) // col_blocks


def gather_kernel(
    density_ref, margin_ref, functions_ref, kind_ref, offset_ref, exponents_ref,
    product_ref, near_out, pops_out,
    dens, marg, around, near_ref, bounds, pops_home, pops_mine, pops_rows,
    sem_spread, got_mine, sem_rows, got_rows, sem_around, got_around, sem_piece, sem_ring, sem_pair, got_slab, got_pair,
    sem_strip, sem_y, sem_half, got_strip, got_half,
):
    row = lax.axis_index("row")
    col = lax.axis_index("col")
    layer = lax.axis_index("layer")
    n_row = lax.axis_size("row")
    n_col = lax.axis_size("col")
    n_layer = lax.axis_size("layer")
    share, strip = marg.shape[1], marg.shape[2]
    slab = dens.shape[1] // 2
    y, x = row // 2, row % 2
    part = layer % 2
    live = col < wanted_cols(n_row * dens.shape[1] // BLK, margin_ref.shape[1] // BLK)
    rows_of = (n_row, marg.shape[0] - n_row)
    cols_of = (n_col, dens.shape[0] - n_col)

    def remote(source, target, sent, got, device):
        return pltpu.make_async_remote_copy(
            src_ref=source, dst_ref=target, send_sem=sent, recv_sem=got,
            device_id=device, device_id_type=MESH,
        )

    def when(condition, body):
        pl.when(condition)(body)

    shifts = [
        (dr, dc, dl) for dl in (-1, 0, 1) for dc in (-1, 0, 1) for dr in (-1, 0, 1)
    ]
    plane = [(0, 2), (1, 2), (0, 3), (1, 3), (0, 0), (0, 1), (1, 0), (1, 1)]
    home_col, home_layer = row // n_layer, row % n_layer
    home = (col == home_col) & (layer == home_layer)
    members = n_col * n_layer
    up, down = ((row + 2) % n_row, col, layer), ((row + n_row - 2) % n_row, col, layer)
    onward, back = (row, (col + 1) % n_col, layer), (row, (col + n_col - 1) % n_col, layer)
    partner = (row, col, layer + 1 - 2 * part)

    def shifted(shift):
        return (
            (row + shift[0] + n_row) % n_row,
            (col + shift[1] + n_col) % n_col,
            (layer + shift[2] + n_layer) % n_layer,
        )

    barrier = pltpu.get_barrier_semaphore()
    for shift in shifts:
        if shift != (0, 0, 0):
            pl.semaphore_signal(barrier, inc=1, device_id=shifted(shift), device_id_type=MESH)
    for device in (up, down):
        pl.semaphore_signal(barrier, inc=1, device_id=device, device_id_type=MESH)
    for xx in range(2):
        for step in range(n_layer):
            if (xx, step) != (0, 0):
                device = (2 * y + (x + xx) % 2, col, (layer + step) % n_layer)
                pl.semaphore_signal(barrier, inc=1, device_id=device, device_id_type=MESH)
    for step in range(1, n_row):
        device = ((row + step) % n_row, col, layer)
        pl.semaphore_signal(barrier, inc=1, device_id=device, device_id_type=MESH)

    lane = lax.broadcasted_iota(jnp.int32, near_ref.shape, 1)
    values = jnp.where(lane == 0, exponents_ref[kind_ref[0]], 0.0)
    for dim in range(3):
        values = jnp.where(lane == dim + 1, offset_ref[dim, 0], values)
    near_ref[...] = values

    @pl.when(home)
    def _():
        atoms = functions_ref.shape[1]
        functions = jnp.broadcast_to(functions_ref[...].astype(jnp.float32), (8, atoms))
        square = (atoms, atoms)
        before = lax.broadcasted_iota(jnp.int32, square, 0) < lax.broadcasted_iota(
            jnp.int32, square, 1
        )
        starts = jnp.dot(
            functions.astype(jnp.bfloat16),
            jnp.where(before, 1.0, 0.0).astype(jnp.bfloat16),
            preferred_element_type=jnp.float32,
        )
        bounds[0] = starts
        bounds[1] = starts + functions

    @pl.when(home)
    def _():
        pl.semaphore_wait(barrier, 26 + 2 + 7 + n_row - 1 + members - 1)

    @pl.when(jnp.logical_not(home))
    def _():
        device = (row, home_col, home_layer)
        pl.semaphore_signal(barrier, inc=1, device_id=device, device_id_type=MESH)
        pl.semaphore_wait(barrier, 26 + 2 + 7 + n_row - 1)

    def piece_copy(kind, target_layer, start):
        slot = dens.at[kind * n_col + col, pl.ds(slab * (target_layer % 2), slab)]
        source = density_ref.at[pl.ds(slab * (target_layer % 2), slab)]
        sent, got = sem_piece.at[target_layer], got_slab.at[kind * n_col + col]
        here = layer == target_layer
        far = remote(source, slot, sent, got, (row, col, target_layer))
        if start:
            when(here, pltpu.make_async_copy(source, slot, got).start)
        when(jnp.logical_not(here), far.start if start else far.wait_send)

    def strip_copy(kind, target, start):
        other, ll = target
        xx = (x + other) % 2
        slot = marg.at[kind * n_row + row]
        source = margin_ref.at[:, pl.ds(strip * ll, strip)]
        sent, got = sem_strip.at[ll * 2 + other], got_strip.at[kind * n_row + row]
        here = (layer == ll) & (other == 0)
        far = remote(source, slot, sent, got, (2 * y + xx, col, ll))
        if start and other == 0:
            when(here, pltpu.make_async_copy(source, slot, got).start)
        when(jnp.logical_not(here), far.start if start else far.wait_send)

    def first_copies(start):
        for kind in range(2):

            def pieces(kind=kind):
                for ll in (2, 3, 0, 1):
                    piece_copy(kind, ll, start)

            def strips(kind=kind):
                for target in plane:
                    strip_copy(kind, target, start)

            when((layer == kind) & (col < cols_of[kind]), pieces)
            when((layer == kind) & (row < rows_of[kind]) & live, strips)

    def around_copy(index):
        dr, dc, dl = shifts[index]
        return remote(
            near_ref, around.at[26 - index], sem_around.at[index], got_around.at[26 - index],
            shifted(shifts[index]),
        )

    def slab_of(kind, origin, half):
        return dens.at[kind * n_col + origin, pl.ds(pl.multiple_of(slab * half, slab), slab)]

    def ring_copy(kind, origin, way, step):
        block = slab_of(kind, origin, part)
        return remote(
            block, block, sem_ring.at[kind, way, step], got_slab.at[kind * n_col + origin],
            (onward, back)[way],
        )

    def pair_copy(kind, origin):
        block = slab_of(kind, origin, part)
        return remote(
            block, block, sem_pair.at[kind * n_col + origin],
            got_pair.at[kind * n_col + origin], partner,
        )

    def pair_wait(kind, origin):
        block = slab_of(kind, origin, 1 - part)
        remote(
            block, block, sem_pair.at[kind * n_col + origin],
            got_pair.at[kind * n_col + origin], partner,
        ).wait_recv()

    def ring_step(step, start):
        half = n_col // 2
        for way in ((0, 1) if step and step < half else (0,)):
            origin = (col + (n_col - step if way == 0 else step)) % n_col
            for kind in range(2):

                def body(kind=kind, origin=origin, way=way):
                    if start:
                        ring_copy(kind, origin, way, 0).wait_recv()
                    sends = [pair_copy(kind, origin)]
                    if way == 0 and step < half:
                        sends.append(ring_copy(kind, origin, 0, step))
                    if step == 0 or (way == 1 and step < half - 1):
                        sends.append(ring_copy(kind, origin, 1, step))
                    for copy in reversed(sends):
                        if start:
                            copy.start()
                        else:
                            copy.wait_send()

                when(origin < cols_of[kind], body)

    def own_strip(kind, other, start):
        origin = 2 * y + (x + other) % 2
        block = marg.at[kind * n_row + origin]
        got = got_strip.at[kind * n_row + origin]

        def body():
            if start:
                remote(block, block, sem_y.at[kind, other, 0], got, up).wait_recv()
            for way in range(2):
                copy = remote(block, block, sem_y.at[kind, other, way], got, (up, down)[way])
                send = copy.start if start else copy.wait_send
                if kind == 1 and way == 1:
                    when(y == 0, send)
                else:
                    send()

        when(live & (origin < rows_of[kind]), body)

    def next_strip(kind, other, way, start):
        origin_y = (y + (3 if way == 0 else 1)) % 4
        origin = 2 * origin_y + (x + other) % 2
        whole = marg.at[kind * n_row + origin]
        block = marg.at[kind * n_row + origin, pl.ds(share // 2 * way, share // 2)]

        def body():
            if start:
                remote(
                    whole, whole, sem_y.at[kind, other, way],
                    got_strip.at[kind * n_row + origin], up,
                ).wait_recv()
            sent = sem_half.at[kind, other, way]
            if kind == 0:
                copy = remote(
                    block, block, sent, got_half.at[origin, way], (up, down)[way]
                )
                (copy.start if start else copy.wait_send)()
            else:
                copy = remote(
                    whole, whole, sent, got_strip.at[n_row + origin], (up, down)[way]
                )
                when(y == (2, 3)[way], copy.start if start else copy.wait_send)

        if kind == 0:
            when(live, body)
        elif way == 0:
            when(live & (origin_y < 2), body)
        else:
            when(live & (origin_y == 0), body)

    def far_strip(kind, xx):
        origin = 2 * ((y + 2) % 4) + xx

        def halves():
            for way in range(2):
                block = marg.at[origin, pl.ds(share // 2 * way, share // 2)]
                remote(
                    block, block, sem_half.at[kind, xx, way], got_half.at[origin, way], up
                ).wait_recv()

        def whole():
            block = marg.at[n_row + origin]
            remote(
                block, block, sem_half.at[kind, xx, 0], got_strip.at[n_row + origin], up
            ).wait_recv()

        if kind == 0:
            when(live, halves)
        else:
            when(live & (y >= 2), whole)

    def nexts(kind, other, start):
        for way in range(2):
            next_strip(kind, other, way, start)

    def relays_low(start):
        ring_step(0, start)
        own_strip(0, 0, start)
        own_strip(1, 0, start)
        ring_step(1, start)
        ring_step(2, start)
        nexts(0, 0, start)
        ring_step(3, start)
        ring_step(4, start)
        nexts(1, 0, start)
        ring_step(5, start)
        ring_step(6, start)
        own_strip(0, 1, start)
        ring_step(7, start)
        ring_step(8, start)
        own_strip(1, 1, start)
        nexts(0, 1, start)
        nexts(1, 1, start)

    def relays_high(start):
        ring_step(0, start)
        ring_step(1, start)
        own_strip(0, 1, start)
        ring_step(2, start)
        own_strip(0, 0, start)
        ring_step(3, start)
        own_strip(1, 1, start)
        ring_step(4, start)
        own_strip(1, 0, start)
        ring_step(5, start)
        ring_step(6, start)
        nexts(0, 1, start)
        ring_step(7, start)
        nexts(0, 0, start)
        ring_step(8, start)
        nexts(1, 1, start)
        nexts(1, 0, start)

    def relays(start):
        when(layer < 2, lambda: relays_low(start))
        when(layer >= 2, lambda: relays_high(start))

    def spread_copy(index):
        return remote(
            pops_home, pops_mine, sem_spread.at[index], got_mine,
            (row, index // n_layer, index % n_layer),
        )

    def row_copies(source):
        return [
            remote(
                source, pops_rows.at[row], sem_rows.at[step], got_rows.at[row],
                ((row + step) % n_row, col, layer),
            )
            for step in range(1, n_row)
        ]

    def spread_step(start):
        def body(step, carry):
            copy = spread_copy((col * n_layer + layer + step) % members)
            if start:
                copy.start()
            else:
                copy.wait_send()
            return carry

        lax.fori_loop(1, members, body, 0)

    first_copies(True)
    for index in range(27):
        if index != 13:
            around_copy(index).start()
    relays(True)
    for kind in range(2):
        for origin in range(cols_of[kind]):
            pair_wait(kind, origin)
        for xx in range(2):
            far_strip(kind, xx)

    @pl.when(live)
    def _():
        product_ref[...] = jnp.zeros_like(product_ref)

        def add_share(j, carry):
            for side in range(2):
                product_ref[...] += jnp.dot(
                    dens[2 * j + side],
                    marg[j, pl.ds(share // 2 * side, share // 2)],
                    preferred_element_type=jnp.float32,
                )
            return carry

        shares = marg.shape[0] - jnp.where(y == 0, 2, 0)
        lax.fori_loop(0, shares, add_share, 0)

    @pl.when(jnp.logical_not(live))
    def _():
        product_ref[...] = jnp.zeros_like(product_ref)

    @pl.when(home)
    def _():
        side = product_ref.shape
        here = lax.broadcasted_iota(jnp.int32, side, 0) == lax.broadcasted_iota(jnp.int32, side, 1)
        diagonal = jnp.sum(jnp.where(here, product_ref[...], 0.0), axis=1, keepdims=True)
        wide = (side[0], functions_ref.shape[1])
        function = lax.broadcasted_iota(jnp.int32, wide, 0) + row * side[0]
        function = function.astype(jnp.float32)
        member = (function >= bounds[0, 0:1, :]) & (function < bounds[1, 0:1, :])
        pops_home[...] = jnp.sum(jnp.where(member, diagonal, 0.0), axis=0, keepdims=True)

    for index in range(27):
        if index != 13:
            around_copy(26 - index).wait_recv()
            near_out[index] = around[index]
    near_out[13] = near_ref[...]

    @pl.when(home)
    def _():
        for copy in row_copies(pops_home):
            copy.start()
        spread_step(True)

    @pl.when(jnp.logical_not(home))
    def _():
        spread_copy(0).wait_recv()
        for copy in row_copies(pops_mine):
            copy.start()

    first_copies(False)
    for index in range(27):
        if index != 13:
            around_copy(index).wait_send()
    relays(False)
    for step in range(1, n_row):
        mate = (row + step) % n_row
        slot = pops_rows.at[mate]
        remote(slot, slot, sem_rows.at[0], got_rows.at[mate], (mate, col, layer)).wait_recv()

    @pl.when(home)
    def _():
        pops_out[...] = pops_home[...]
        spread_step(False)

    @pl.when(jnp.logical_not(home))
    def _():
        pops_out[...] = pops_mine[...]

    for step in range(1, n_row):
        pops_out[...] += pops_rows[(row + step) % n_row]
    for copy in row_copies(pops_mine):
        copy.wait_send()


def gather_product(density, margin, functions, kind, offset, exponents):
    rows_here, piece_width = density.shape
    share, share_cols = margin.shape
    n_row, n_col, n_layer = (lax.axis_size(axis) for axis in ("row", "col", "layer"))
    depth = n_row * rows_here + REACH * BLK
    strip = share_cols // n_layer
    dma = pltpu.SemaphoreType.DMA
    near, atoms = (1, 128), functions.shape[0]
    vmem = pl.BlockSpec(memory_space=pltpu.VMEM)
    smem = pl.BlockSpec(memory_space=pltpu.SMEM)
    anywhere = pl.BlockSpec(memory_space=pl.ANY)
    pieces, shares = depth // piece_width, depth // share
    return pl.pallas_call(
        gather_kernel,
        out_shape=(
            jax.ShapeDtypeStruct((rows_here, strip), jnp.float32),
            jax.ShapeDtypeStruct((27,) + near, jnp.float32),
            jax.ShapeDtypeStruct((1, atoms), jnp.float32),
        ),
        in_specs=[anywhere, anywhere, vmem, smem, smem, smem],
        out_specs=(vmem, vmem, vmem),
        scratch_shapes=[
            pltpu.VMEM((pieces, rows_here, piece_width), jnp.bfloat16),
            pltpu.VMEM((shares, share, strip), jnp.bfloat16),
            pltpu.VMEM((27,) + near, jnp.float32),
            pltpu.VMEM(near, jnp.float32),
            pltpu.VMEM((2, 8, atoms), jnp.float32),
            pltpu.VMEM((1, atoms), jnp.float32),
            pltpu.VMEM((1, atoms), jnp.float32),
            pltpu.VMEM((n_row, 1, atoms), jnp.float32),
            dma((n_col * n_layer,)),
            dma,
            dma((n_row,)),
            dma((n_row,)),
            dma((27,)),
            dma((27,)),
            dma((n_layer,)),
            dma((2, 2, n_col // 2)),
            dma((pieces,)),
            dma((pieces,)),
            dma((pieces,)),
            dma((2 * n_layer,)),
            dma((2, 2, 2)),
            dma((2, 2, 2)),
            dma((shares,)),
            dma((n_row, 2)),
        ],
        compiler_params=pltpu.CompilerParams(
            collective_id=1, has_side_effects=True, vmem_limit_bytes=24 * 1024 * 1024
        ),
    )(density, margin, functions.reshape(1, -1), kind, offset, exponents)


def near_profile(cells, tile_of, extent, offset, exponent_of):
    local = jnp.arange(cells, dtype=jnp.int32)[None, :] - tile_of[:, None] * extent
    distance = local.astype(jnp.float32) - offset[:, None]
    return jnp.where(
        jnp.abs(distance) <= HALO, jnp.exp(-exponent_of[:, None] * distance * distance), 0.0
    )


def collocate(near, weights):
    index = jnp.arange(27, dtype=jnp.int32)
    exponent_of = near[:, 0]
    along_x = near_profile(TX, index % 3 - 1, TX, near[:, 1], exponent_of)
    along_y = near_profile(TY, index // 3 % 3 - 1, TY, near[:, 2], exponent_of)
    along_z = near_profile(TZ, index // 9 - 1, TZ, near[:, 3], exponent_of)
    paired = (weights[:, None] * along_x)[:, :, None] * along_y[:, None, :]
    return jnp.einsum("axy,az->xyz", paired, along_z, precision=lax.Precision.HIGHEST)


def shards(density, margin, block_pattern, atom_functions, atom_kind, atom_offset, exponents):
    rows_here, piece_width = density.shape
    share_rows, share_cols = margin.shape
    n_row = lax.axis_size("row")
    n_col = lax.axis_size("col")
    n_layer = lax.axis_size("layer")
    row_index = lax.axis_index("row")
    col_index = lax.axis_index("col")
    layer_index = lax.axis_index("layer")
    density_mask = lax.dynamic_slice(
        block_pattern,
        (row_index * (rows_here // BLK), (layer_index * n_col + col_index) * piece_width // BLK),
        (rows_here // BLK, piece_width // BLK),
    )
    masked = apply_pattern(density, density_mask)
    margin_mask = lax.dynamic_slice(
        block_pattern,
        ((layer_index * n_row + row_index) * share_rows // BLK, col_index * share_cols // BLK),
        (share_rows // BLK, share_cols // BLK),
    )
    margin_masked = apply_pattern(margin, margin_mask)
    product, near_all, pops = gather_product(
        masked, margin_masked, atom_functions, atom_kind, atom_offset, exponents
    )
    near = near_all[:, 0, :4]
    all_pop = pops.reshape(-1)
    index = jnp.arange(27, dtype=jnp.int32)
    near_atom = (
        ((row_index + index % 3 - 1) % n_row) * n_col + (col_index + index // 3 % 3 - 1) % n_col
    ) * n_layer + (layer_index + index // 9 - 1) % n_layer
    atoms = jnp.arange(all_pop.shape[0], dtype=jnp.int32)
    weights = jnp.sum(jnp.where(near_atom[:, None] == atoms[None, :], all_pop[None, :], 0.0), axis=1)
    return (product.astype(jnp.bfloat16), collocate(near, weights))


def apply_pattern(matrix, pattern_part):
    row_blocks = matrix.shape[0] // BLK
    col_blocks = matrix.shape[1] // BLK
    shaped = matrix.reshape(row_blocks, BLK, col_blocks, BLK)
    gate_mask = pattern_part.astype(jnp.bfloat16)
    return (shaped * gate_mask[:, None, :, None]).reshape(matrix.shape)


def shards(density, margin, block_pattern, atom_functions, atom_kind, atom_offset, exponents):
    rows_here, piece_width = density.shape
    share_rows, share_cols = margin.shape
    n_row = lax.axis_size("row")
    n_col = lax.axis_size("col")
    n_layer = lax.axis_size("layer")
    row_index = lax.axis_index("row")
    col_index = lax.axis_index("col")
    layer_index = lax.axis_index("layer")
    density_mask = lax.dynamic_slice(
        block_pattern,
        (row_index * (rows_here // BLK), (layer_index * n_col + col_index) * piece_width // BLK),
        (rows_here // BLK, piece_width // BLK),
    )
    masked = apply_pattern(density, density_mask)
    margin_mask = lax.dynamic_slice(
        block_pattern,
        ((layer_index * n_row + row_index) * share_rows // BLK, col_index * share_cols // BLK),
        (share_rows // BLK, share_cols // BLK),
    )
    margin_masked = apply_pattern(margin, margin_mask)
    product, near_all, pops = gather_product(
        masked, margin_masked, atom_functions, atom_kind, atom_offset, exponents
    )
    near = near_all[:, 0, :4]
    all_pop = pops.reshape(-1)
    index = jnp.arange(27, dtype=jnp.int32)
    near_atom = (
        ((row_index + index % 3 - 1) % n_row) * n_col + (col_index + index // 3 % 3 - 1) % n_col
    ) * n_layer + (layer_index + index // 9 - 1) % n_layer
    atoms = jnp.arange(all_pop.shape[0], dtype=jnp.int32)
    weights = jnp.sum(jnp.where(near_atom[:, None] == atoms[None, :], all_pop[None, :], 0.0), axis=1)
    return (product.astype(jnp.bfloat16), collocate(near, weights))


def apply_pattern(matrix, pattern_part):
    row_blocks = matrix.shape[0] // BLK
    col_blocks = matrix.shape[1] // BLK
    shaped = matrix.reshape(row_blocks, BLK, col_blocks, BLK)
    gate_mask = pattern_part.astype(jnp.bfloat16)
    return (shaped * gate_mask[:, None, :, None]).reshape(matrix.shape)


def kind_exponent(kinds_of, exponents):
    kind_match = kinds_of[:, None] == jnp.arange(exponents.shape[0], dtype=jnp.int32)[None, :]
    return jnp.sum(jnp.where(kind_match, exponents[None, :], 0.0), axis=1)


def solution(mesh):
    placed = (
        P("row", ("layer", "col")),
        P(("layer", "row"), "col"),
        P(),
        P(),
        P(("row", "col", "layer")),
        P(None, ("row", "col", "layer")),
        P(),
    )
    return jax.shard_map(
        shards,
        mesh=mesh,
        in_specs=placed,
        out_specs=(P("row", ("col", "layer")), P("row", "col", "layer")),
        check_vma=False,
    )
```

```python
import jax
import jax.numpy as jnp
from jax import lax
from jax.experimental import pallas as pl
from jax.experimental.pallas import tpu as pltpu
from jax.sharding import PartitionSpec as P

BLK = 128
TX = 32
TY = 32
TZ = 128
HALO = 16

MESH = pl.DeviceIdType.MESH


REACH = 32


def wanted_cols(window_blocks, col_blocks):
    return (window_blocks + 2 * REACH + col_blocks - 1) // col_blocks


def gather_kernel(
    density_ref, margin_ref, functions_ref, kind_ref, offset_ref, exponents_ref,
    product_ref, near_out, pops_out,
    dens, marg, hops, sem_hop, got_hop, sem_onto, around, near_ref, bounds, pops_home, pops_mine, pops_rows,
    sem_spread, got_mine, sem_rows, got_rows, sem_around, got_around, sem_piece, sem_ring, sem_pair, got_slab, got_pair,
    sem_strip, sem_y, sem_half, got_strip, got_half,
):
    row = lax.axis_index("row")
    col = lax.axis_index("col")
    layer = lax.axis_index("layer")
    n_row = lax.axis_size("row")
    n_col = lax.axis_size("col")
    n_layer = lax.axis_size("layer")
    share, strip = marg.shape[1], marg.shape[2]
    slab = dens.shape[1] // 2
    y, x = row // 2, row % 2
    part = layer % 2
    live = col < wanted_cols(n_row * dens.shape[1] // BLK, margin_ref.shape[1] // BLK)
    rows_of = (n_row, marg.shape[0] - n_row)
    cols_of = (n_col, dens.shape[0] - n_col)

    def remote(source, target, sent, got, device):
        return pltpu.make_async_remote_copy(
            src_ref=source, dst_ref=target, send_sem=sent, recv_sem=got,
            device_id=device, device_id_type=MESH,
        )

    def when(condition, body):
        pl.when(condition)(body)

    shifts = [
        (dr, dc, dl) for dl in (-1, 0, 1) for dc in (-1, 0, 1) for dr in (-1, 0, 1)
    ]
    plane = [(0, 2), (1, 2), (0, 3), (1, 3), (0, 0), (0, 1)]
    home_col, home_layer = row // n_layer, row % n_layer
    home = (col == home_col) & (layer == home_layer)
    members = n_col * n_layer
    up, down = ((row + 2) % n_row, col, layer), ((row + n_row - 2) % n_row, col, layer)
    onward, back = (row, (col + 1) % n_col, layer), (row, (col + n_col - 1) % n_col, layer)
    partner = (row, col, layer + 1 - 2 * part)

    def shifted(shift):
        return (
            (row + shift[0] + n_row) % n_row,
            (col + shift[1] + n_col) % n_col,
            (layer + shift[2] + n_layer) % n_layer,
        )

    barrier = pltpu.get_barrier_semaphore()
    for shift in shifts:
        if shift != (0, 0, 0):
            pl.semaphore_signal(barrier, inc=1, device_id=shifted(shift), device_id_type=MESH)
    for device in (up, down):
        pl.semaphore_signal(barrier, inc=1, device_id=device, device_id_type=MESH)
    for xx in range(2):
        for step in range(n_layer):
            if (xx, step) != (0, 0):
                device = (2 * y + (x + xx) % 2, col, (layer + step) % n_layer)
                pl.semaphore_signal(barrier, inc=1, device_id=device, device_id_type=MESH)
    for step in range(1, n_row):
        device = ((row + step) % n_row, col, layer)
        pl.semaphore_signal(barrier, inc=1, device_id=device, device_id_type=MESH)

    lane = lax.broadcasted_iota(jnp.int32, near_ref.shape, 1)
    values = jnp.where(lane == 0, exponents_ref[kind_ref[0]], 0.0)
    for dim in range(3):
        values = jnp.where(lane == dim + 1, offset_ref[dim, 0], values)
    near_ref[...] = values

    @pl.when(home)
    def _():
        atoms = functions_ref.shape[1]
        functions = jnp.broadcast_to(functions_ref[...].astype(jnp.float32), (8, atoms))
        square = (atoms, atoms)
        before = lax.broadcasted_iota(jnp.int32, square, 0) < lax.broadcasted_iota(
            jnp.int32, square, 1
        )
        starts = jnp.dot(
            functions.astype(jnp.bfloat16),
            jnp.where(before, 1.0, 0.0).astype(jnp.bfloat16),
            preferred_element_type=jnp.float32,
        )
        bounds[0] = starts
        bounds[1] = starts + functions

    @pl.when(home)
    def _():
        pl.semaphore_wait(barrier, 26 + 2 + 7 + n_row - 1 + members - 1)

    @pl.when(jnp.logical_not(home))
    def _():
        device = (row, home_col, home_layer)
        pl.semaphore_signal(barrier, inc=1, device_id=device, device_id_type=MESH)
        pl.semaphore_wait(barrier, 26 + 2 + 7 + n_row - 1)

    def piece_copy(kind, target_layer, start):
        slot = dens.at[kind * n_col + col, pl.ds(slab * (target_layer % 2), slab)]
        source = density_ref.at[pl.ds(slab * (target_layer % 2), slab)]
        sent, got = sem_piece.at[target_layer], got_slab.at[kind * n_col + col]
        here = layer == target_layer
        far = remote(source, slot, sent, got, (row, col, target_layer))
        if start:
            when(here, pltpu.make_async_copy(source, slot, got).start)
        when(jnp.logical_not(here), far.start if start else far.wait_send)

    def strip_copy(kind, target, start):
        other, ll = target
        xx = (x + other) % 2
        slot = marg.at[kind * n_row + row]
        source = margin_ref.at[:, pl.ds(strip * ll, strip)]
        sent, got = sem_strip.at[ll * 2 + other], got_strip.at[kind * n_row + row]
        here = (layer == ll) & (other == 0)
        far = remote(source, slot, sent, got, (2 * y + xx, col, ll))
        if start and other == 0:
            when(here, pltpu.make_async_copy(source, slot, got).start)
        when(jnp.logical_not(here), far.start if start else far.wait_send)

    def hop_copy(kind, ll, side, start):
        slot = 2 * kind + x
        far = remote(
            margin_ref.at[pl.ds(share // 2 * side, share // 2), pl.ds(strip * ll, strip)],
            hops.at[slot], sem_hop.at[ll, side], got_hop.at[slot],
            (2 * y + (x + side) % 2, col, 2 + ll),
        )
        (far.start if start else far.wait_send)()

    def hop_onto(kind, side, start):
        origin = (x + side) % 2
        slot = 2 * kind + origin
        block = hops.at[slot]

        def body():
            target = marg.at[
                kind * n_row + 2 * y + origin, pl.ds(share // 2 * side, share // 2)
            ]
            copy = remote(
                block, target, sem_onto.at[slot], got_strip.at[kind * n_row + 2 * y + origin],
                (2 * y + 1 - origin, col, layer - 2),
            )
            if start:
                remote(block, block, sem_onto.at[slot], got_hop.at[slot], up).wait_recv()
                copy.start()
            else:
                copy.wait_send()

        when(live & (2 * y + origin < rows_of[kind]), body)

    def first_copies(start):
        for kind in range(2):

            def pieces(kind=kind):
                for ll in (2, 3, 0, 1):
                    piece_copy(kind, ll, start)

            def strips(kind=kind):
                for ll in range(2):
                    for side in range(2):
                        hop_copy(kind, ll, side, start)
                for target in plane:
                    strip_copy(kind, target, start)

            when((layer == kind) & (col < cols_of[kind]), pieces)
            when((layer == kind) & (row < rows_of[kind]) & live, strips)

    def around_copy(index):
        dr, dc, dl = shifts[index]
        return remote(
            near_ref, around.at[26 - index], sem_around.at[index], got_around.at[26 - index],
            shifted(shifts[index]),
        )

    def slab_of(kind, origin, half):
        return dens.at[kind * n_col + origin, pl.ds(pl.multiple_of(slab * half, slab), slab)]

    def ring_copy(kind, origin, way, step):
        block = slab_of(kind, origin, part)
        return remote(
            block, block, sem_ring.at[kind, way, step], got_slab.at[kind * n_col + origin],
            (onward, back)[way],
        )

    def pair_copy(kind, origin):
        block = slab_of(kind, origin, part)
        return remote(
            block, block, sem_pair.at[kind * n_col + origin],
            got_pair.at[kind * n_col + origin], partner,
        )

    def pair_wait(kind, origin):
        block = slab_of(kind, origin, 1 - part)
        remote(
            block, block, sem_pair.at[kind * n_col + origin],
            got_pair.at[kind * n_col + origin], partner,
        ).wait_recv()

    def ring_step(step, start):
        half = n_col // 2
        for way in ((0, 1) if step and step < half else (0,)):
            origin = (col + (n_col - step if way == 0 else step)) % n_col
            for kind in range(2):

                def body(kind=kind, origin=origin, way=way):
                    if start:
                        ring_copy(kind, origin, way, 0).wait_recv()
                    sends = [pair_copy(kind, origin)]
                    if way == 0 and step < half:
                        sends.append(ring_copy(kind, origin, 0, step))
                    if step == 0 or (way == 1 and step < half - 1):
                        sends.append(ring_copy(kind, origin, 1, step))
                    for copy in reversed(sends):
                        if start:
                            copy.start()
                        else:
                            copy.wait_send()

                when(origin < cols_of[kind], body)

    def own_strip(kind, other, start):
        origin = 2 * y + (x + other) % 2
        block = marg.at[kind * n_row + origin]
        got = got_strip.at[kind * n_row + origin]

        def body():
            if start:
                remote(block, block, sem_y.at[kind, other, 0], got, up).wait_recv()
            for way in range(2):
                copy = remote(block, block, sem_y.at[kind, other, way], got, (up, down)[way])
                send = copy.start if start else copy.wait_send
                if kind == 1 and way == 1:
                    when(y == 0, send)
                else:
                    send()

        when(live & (origin < rows_of[kind]), body)

    def next_strip(kind, other, way, start):
        origin_y = (y + (3 if way == 0 else 1)) % 4
        origin = 2 * origin_y + (x + other) % 2
        whole = marg.at[kind * n_row + origin]
        block = marg.at[kind * n_row + origin, pl.ds(share // 2 * way, share // 2)]

        def body():
            if start:
                remote(
                    whole, whole, sem_y.at[kind, other, way],
                    got_strip.at[kind * n_row + origin], up,
                ).wait_recv()
            sent = sem_half.at[kind, other, way]
            if kind == 0:
                copy = remote(
                    block, block, sent, got_half.at[origin, way], (up, down)[way]
                )
                (copy.start if start else copy.wait_send)()
            else:
                copy = remote(
                    whole, whole, sent, got_strip.at[n_row + origin], (up, down)[way]
                )
                when(y == (2, 3)[way], copy.start if start else copy.wait_send)

        if kind == 0:
            when(live, body)
        elif way == 0:
            when(live & (origin_y < 2), body)
        else:
            when(live & (origin_y == 0), body)

    def far_strip(kind, xx):
        origin = 2 * ((y + 2) % 4) + xx

        def halves():
            for way in range(2):
                block = marg.at[origin, pl.ds(share // 2 * way, share // 2)]
                remote(
                    block, block, sem_half.at[kind, xx, way], got_half.at[origin, way], up
                ).wait_recv()

        def whole():
            block = marg.at[n_row + origin]
            remote(
                block, block, sem_half.at[kind, xx, 0], got_strip.at[n_row + origin], up
            ).wait_recv()

        if kind == 0:
            when(live, halves)
        else:
            when(live & (y >= 2), whole)

    def nexts(kind, other, start):
        for way in range(2):
            next_strip(kind, other, way, start)

    def relays_low(start):
        ring_step(0, start)
        own_strip(0, 0, start)
        own_strip(1, 0, start)
        ring_step(1, start)
        ring_step(2, start)
        nexts(0, 0, start)
        ring_step(3, start)
        own_strip(0, 1, start)
        ring_step(4, start)
        nexts(1, 0, start)
        own_strip(1, 1, start)
        ring_step(5, start)
        ring_step(6, start)
        ring_step(7, start)
        ring_step(8, start)
        nexts(0, 1, start)
        nexts(1, 1, start)

    def relays_high(start):
        ring_step(0, start)
        hop_onto(0, 0, start)
        hop_onto(0, 1, start)
        ring_step(1, start)
        hop_onto(1, 0, start)
        hop_onto(1, 1, start)
        own_strip(0, 1, start)
        ring_step(2, start)
        own_strip(0, 0, start)
        ring_step(3, start)
        own_strip(1, 1, start)
        ring_step(4, start)
        own_strip(1, 0, start)
        ring_step(5, start)
        ring_step(6, start)
        nexts(0, 1, start)
        ring_step(7, start)
        nexts(0, 0, start)
        ring_step(8, start)
        nexts(1, 1, start)
        nexts(1, 0, start)

    def relays(start):
        when(layer < 2, lambda: relays_low(start))
        when(layer >= 2, lambda: relays_high(start))

    def spread_copy(index):
        return remote(
            pops_home, pops_mine, sem_spread.at[index], got_mine,
            (row, index // n_layer, index % n_layer),
        )

    def row_copies(source):
        return [
            remote(
                source, pops_rows.at[row], sem_rows.at[step], got_rows.at[row],
                ((row + step) % n_row, col, layer),
            )
            for step in range(1, n_row)
        ]

    def spread_step(start):
        def body(step, carry):
            copy = spread_copy((col * n_layer + layer + step) % members)
            if start:
                copy.start()
            else:
                copy.wait_send()
            return carry

        lax.fori_loop(1, members, body, 0)

    first_copies(True)
    for index in range(27):
        if index != 13:
            around_copy(index).start()
    relays(True)
    for kind in range(2):
        for origin in range(cols_of[kind]):
            pair_wait(kind, origin)
        for xx in range(2):
            far_strip(kind, xx)

    @pl.when(live)
    def _():
        product_ref[...] = jnp.zeros_like(product_ref)

        def add_share(j, carry):
            for side in range(2):
                product_ref[...] += jnp.dot(
                    dens[2 * j + side],
                    marg[j, pl.ds(share // 2 * side, share // 2)],
                    preferred_element_type=jnp.float32,
                )
            return carry

        shares = marg.shape[0] - jnp.where(y == 0, 2, 0)
        lax.fori_loop(0, shares, add_share, 0)

    @pl.when(jnp.logical_not(live))
    def _():
        product_ref[...] = jnp.zeros_like(product_ref)

    @pl.when(home)
    def _():
        side = product_ref.shape
        here = lax.broadcasted_iota(jnp.int32, side, 0) == lax.broadcasted_iota(jnp.int32, side, 1)
        diagonal = jnp.sum(jnp.where(here, product_ref[...], 0.0), axis=1, keepdims=True)
        wide = (side[0], functions_ref.shape[1])
        function = lax.broadcasted_iota(jnp.int32, wide, 0) + row * side[0]
        function = function.astype(jnp.float32)
        member = (function >= bounds[0, 0:1, :]) & (function < bounds[1, 0:1, :])
        pops_home[...] = jnp.sum(jnp.where(member, diagonal, 0.0), axis=0, keepdims=True)

    for index in range(27):
        if index != 13:
            around_copy(26 - index).wait_recv()
            near_out[index] = around[index]
    near_out[13] = near_ref[...]

    @pl.when(home)
    def _():
        for copy in row_copies(pops_home):
            copy.start()
        spread_step(True)

    @pl.when(jnp.logical_not(home))
    def _():
        spread_copy(0).wait_recv()
        for copy in row_copies(pops_mine):
            copy.start()

    first_copies(False)
    for index in range(27):
        if index != 13:
            around_copy(index).wait_send()
    relays(False)
    for step in range(1, n_row):
        mate = (row + step) % n_row
        slot = pops_rows.at[mate]
        remote(slot, slot, sem_rows.at[0], got_rows.at[mate], (mate, col, layer)).wait_recv()

    @pl.when(home)
    def _():
        pops_out[...] = pops_home[...]
        spread_step(False)

    @pl.when(jnp.logical_not(home))
    def _():
        pops_out[...] = pops_mine[...]

    for step in range(1, n_row):
        pops_out[...] += pops_rows[(row + step) % n_row]
    for copy in row_copies(pops_mine):
        copy.wait_send()


def gather_product(density, margin, functions, kind, offset, exponents):
    rows_here, piece_width = density.shape
    share, share_cols = margin.shape
    n_row, n_col, n_layer = (lax.axis_size(axis) for axis in ("row", "col", "layer"))
    depth = n_row * rows_here + REACH * BLK
    strip = share_cols // n_layer
    dma = pltpu.SemaphoreType.DMA
    near, atoms = (1, 128), functions.shape[0]
    vmem = pl.BlockSpec(memory_space=pltpu.VMEM)
    smem = pl.BlockSpec(memory_space=pltpu.SMEM)
    anywhere = pl.BlockSpec(memory_space=pl.ANY)
    pieces, shares = depth // piece_width, depth // share
    return pl.pallas_call(
        gather_kernel,
        out_shape=(
            jax.ShapeDtypeStruct((rows_here, strip), jnp.float32),
            jax.ShapeDtypeStruct((27,) + near, jnp.float32),
            jax.ShapeDtypeStruct((1, atoms), jnp.float32),
        ),
        in_specs=[anywhere, anywhere, vmem, smem, smem, smem],
        out_specs=(vmem, vmem, vmem),
        scratch_shapes=[
            pltpu.VMEM((pieces, rows_here, piece_width), jnp.bfloat16),
            pltpu.VMEM((shares, share, strip), jnp.bfloat16),
            pltpu.VMEM((4, share // 2, strip), jnp.bfloat16),
            dma((2, 2)),
            dma((4,)),
            dma((4,)),
            pltpu.VMEM((27,) + near, jnp.float32),
            pltpu.VMEM(near, jnp.float32),
            pltpu.VMEM((2, 8, atoms), jnp.float32),
            pltpu.VMEM((1, atoms), jnp.float32),
            pltpu.VMEM((1, atoms), jnp.float32),
            pltpu.VMEM((n_row, 1, atoms), jnp.float32),
            dma((n_col * n_layer,)),
            dma,
            dma((n_row,)),
            dma((n_row,)),
            dma((27,)),
            dma((27,)),
            dma((n_layer,)),
            dma((2, 2, n_col // 2)),
            dma((pieces,)),
            dma((pieces,)),
            dma((pieces,)),
            dma((2 * n_layer,)),
            dma((2, 2, 2)),
            dma((2, 2, 2)),
            dma((shares,)),
            dma((n_row, 2)),
        ],
        compiler_params=pltpu.CompilerParams(
            collective_id=1, has_side_effects=True, vmem_limit_bytes=24 * 1024 * 1024
        ),
    )(density, margin, functions.reshape(1, -1), kind, offset, exponents)


def near_profile(cells, tile_of, extent, offset, exponent_of):
    local = jnp.arange(cells, dtype=jnp.int32)[None, :] - tile_of[:, None] * extent
    distance = local.astype(jnp.float32) - offset[:, None]
    return jnp.where(
        jnp.abs(distance) <= HALO, jnp.exp(-exponent_of[:, None] * distance * distance), 0.0
    )


def collocate(near, weights):
    index = jnp.arange(27, dtype=jnp.int32)
    exponent_of = near[:, 0]
    along_x = near_profile(TX, index % 3 - 1, TX, near[:, 1], exponent_of)
    along_y = near_profile(TY, index // 3 % 3 - 1, TY, near[:, 2], exponent_of)
    along_z = near_profile(TZ, index // 9 - 1, TZ, near[:, 3], exponent_of)
    paired = (weights[:, None] * along_x)[:, :, None] * along_y[:, None, :]
    return jnp.einsum("axy,az->xyz", paired, along_z, precision=lax.Precision.HIGHEST)


def shards(density, margin, block_pattern, atom_functions, atom_kind, atom_offset, exponents):
    rows_here, piece_width = density.shape
    share_rows, share_cols = margin.shape
    n_row = lax.axis_size("row")
    n_col = lax.axis_size("col")
    n_layer = lax.axis_size("layer")
    row_index = lax.axis_index("row")
    col_index = lax.axis_index("col")
    layer_index = lax.axis_index("layer")
    density_mask = lax.dynamic_slice(
        block_pattern,
        (row_index * (rows_here // BLK), (layer_index * n_col + col_index) * piece_width // BLK),
        (rows_here // BLK, piece_width // BLK),
    )
    masked = apply_pattern(density, density_mask)
    margin_mask = lax.dynamic_slice(
        block_pattern,
        ((layer_index * n_row + row_index) * share_rows // BLK, col_index * share_cols // BLK),
        (share_rows // BLK, share_cols // BLK),
    )
    margin_masked = apply_pattern(margin, margin_mask)
    product, near_all, pops = gather_product(
        masked, margin_masked, atom_functions, atom_kind, atom_offset, exponents
    )
    near = near_all[:, 0, :4]
    all_pop = pops.reshape(-1)
    index = jnp.arange(27, dtype=jnp.int32)
    near_atom = (
        ((row_index + index % 3 - 1) % n_row) * n_col + (col_index + index // 3 % 3 - 1) % n_col
    ) * n_layer + (layer_index + index // 9 - 1) % n_layer
    atoms = jnp.arange(all_pop.shape[0], dtype=jnp.int32)
    weights = jnp.sum(jnp.where(near_atom[:, None] == atoms[None, :], all_pop[None, :], 0.0), axis=1)
    return (product.astype(jnp.bfloat16), collocate(near, weights))


def apply_pattern(matrix, pattern_part):
    row_blocks = matrix.shape[0] // BLK
    col_blocks = matrix.shape[1] // BLK
    shaped = matrix.reshape(row_blocks, BLK, col_blocks, BLK)
    gate_mask = pattern_part.astype(jnp.bfloat16)
    return (shaped * gate_mask[:, None, :, None]).reshape(matrix.shape)


def shards(density, margin, block_pattern, atom_functions, atom_kind, atom_offset, exponents):
    rows_here, piece_width = density.shape
    share_rows, share_cols = margin.shape
    n_row = lax.axis_size("row")
    n_col = lax.axis_size("col")
    n_layer = lax.axis_size("layer")
    row_index = lax.axis_index("row")
    col_index = lax.axis_index("col")
    layer_index = lax.axis_index("layer")
    density_mask = lax.dynamic_slice(
        block_pattern,
        (row_index * (rows_here // BLK), (layer_index * n_col + col_index) * piece_width // BLK),
        (rows_here // BLK, piece_width // BLK),
    )
    masked = apply_pattern(density, density_mask)
    margin_mask = lax.dynamic_slice(
        block_pattern,
        ((layer_index * n_row + row_index) * share_rows // BLK, col_index * share_cols // BLK),
        (share_rows // BLK, share_cols // BLK),
    )
    margin_masked = apply_pattern(margin, margin_mask)
    product, near_all, pops = gather_product(
        masked, margin_masked, atom_functions, atom_kind, atom_offset, exponents
    )
    near = near_all[:, 0, :4]
    all_pop = pops.reshape(-1)
    index = jnp.arange(27, dtype=jnp.int32)
    near_atom = (
        ((row_index + index % 3 - 1) % n_row) * n_col + (col_index + index // 3 % 3 - 1) % n_col
    ) * n_layer + (layer_index + index // 9 - 1) % n_layer
    atoms = jnp.arange(all_pop.shape[0], dtype=jnp.int32)
    weights = jnp.sum(jnp.where(near_atom[:, None] == atoms[None, :], all_pop[None, :], 0.0), axis=1)
    return (product.astype(jnp.bfloat16), collocate(near, weights))


def apply_pattern(matrix, pattern_part):
    row_blocks = matrix.shape[0] // BLK
    col_blocks = matrix.shape[1] // BLK
    shaped = matrix.reshape(row_blocks, BLK, col_blocks, BLK)
    gate_mask = pattern_part.astype(jnp.bfloat16)
    return (shaped * gate_mask[:, None, :, None]).reshape(matrix.shape)


def kind_exponent(kinds_of, exponents):
    kind_match = kinds_of[:, None] == jnp.arange(exponents.shape[0], dtype=jnp.int32)[None, :]
    return jnp.sum(jnp.where(kind_match, exponents[None, :], 0.0), axis=1)


def solution(mesh):
    placed = (
        P("row", ("layer", "col")),
        P(("layer", "row"), "col"),
        P(),
        P(),
        P(("row", "col", "layer")),
        P(None, ("row", "col", "layer")),
        P(),
    )
    return jax.shard_map(
        shards,
        mesh=mesh,
        in_specs=placed,
        out_specs=(P("row", ("col", "layer")), P("row", "col", "layer")),
        check_vma=False,
    )
```

```python
import jax
import jax.numpy as jnp
from jax import lax
from jax.experimental import pallas as pl
from jax.experimental.pallas import tpu as pltpu
from jax.sharding import PartitionSpec as P

BLK = 128
TX = 32
TY = 32
TZ = 128
HALO = 16

MESH = pl.DeviceIdType.MESH


REACH = 32


def wanted_cols(window_blocks, col_blocks):
    return (window_blocks + 2 * REACH + col_blocks - 1) // col_blocks


def gather_kernel(
    density_ref, margin_ref, functions_ref, kind_ref, offset_ref, exponents_ref,
    product_ref, near_out, pops_out,
    dens, marg, around, near_ref, bounds, pops_home, pops_mine, pops_rows,
    sem_spread, got_mine, sem_rows, got_rows, sem_around, got_around, sem_piece, sem_ring, sem_pair, got_slab, got_pair,
    sem_strip, sem_y, sem_half, got_strip, got_half,
):
    row = lax.axis_index("row")
    col = lax.axis_index("col")
    layer = lax.axis_index("layer")
    n_row = lax.axis_size("row")
    n_col = lax.axis_size("col")
    n_layer = lax.axis_size("layer")
    share, strip = marg.shape[1], marg.shape[2]
    slab = dens.shape[1] // 2
    y, x = row // 2, row % 2
    part = layer % 2
    live = col < wanted_cols(n_row * dens.shape[1] // BLK, margin_ref.shape[1] // BLK)
    rows_of = (n_row, marg.shape[0] - n_row)
    cols_of = (n_col, dens.shape[0] - n_col)

    def remote(source, target, sent, got, device):
        return pltpu.make_async_remote_copy(
            src_ref=source, dst_ref=target, send_sem=sent, recv_sem=got,
            device_id=device, device_id_type=MESH,
        )

    def when(condition, body):
        pl.when(condition)(body)

    shifts = [
        (dr, dc, dl) for dl in (-1, 0, 1) for dc in (-1, 0, 1) for dr in (-1, 0, 1)
    ]
    plane = [(0, 2), (1, 2), (0, 3), (1, 3), (0, 0), (0, 1), (1, 0), (1, 1)]
    home_col, home_layer = row // n_layer, row % n_layer
    home = (col == home_col) & (layer == home_layer)
    members = n_col * n_layer
    up, down = ((row + 2) % n_row, col, layer), ((row + n_row - 2) % n_row, col, layer)
    onward, back = (row, (col + 1) % n_col, layer), (row, (col + n_col - 1) % n_col, layer)
    partner = (row, col, layer + 1 - 2 * part)

    def shifted(shift):
        return (
            (row + shift[0] + n_row) % n_row,
            (col + shift[1] + n_col) % n_col,
            (layer + shift[2] + n_layer) % n_layer,
        )

    barrier = pltpu.get_barrier_semaphore()
    for shift in shifts:
        if shift != (0, 0, 0):
            pl.semaphore_signal(barrier, inc=1, device_id=shifted(shift), device_id_type=MESH)
    for device in (up, down):
        pl.semaphore_signal(barrier, inc=1, device_id=device, device_id_type=MESH)
    for xx in range(2):
        for step in range(n_layer):
            if (xx, step) != (0, 0):
                device = (2 * y + (x + xx) % 2, col, (layer + step) % n_layer)
                pl.semaphore_signal(barrier, inc=1, device_id=device, device_id_type=MESH)
    for step in range(1, n_row):
        device = ((row + step) % n_row, col, layer)
        pl.semaphore_signal(barrier, inc=1, device_id=device, device_id_type=MESH)

    lane = lax.broadcasted_iota(jnp.int32, near_ref.shape, 1)
    values = jnp.where(lane == 0, exponents_ref[kind_ref[0]], 0.0)
    for dim in range(3):
        values = jnp.where(lane == dim + 1, offset_ref[dim, 0], values)
    near_ref[...] = values

    @pl.when(home)
    def _():
        atoms = functions_ref.shape[1]
        functions = jnp.broadcast_to(functions_ref[...].astype(jnp.float32), (8, atoms))
        square = (atoms, atoms)
        before = lax.broadcasted_iota(jnp.int32, square, 0) < lax.broadcasted_iota(
            jnp.int32, square, 1
        )
        starts = jnp.dot(
            functions.astype(jnp.bfloat16),
            jnp.where(before, 1.0, 0.0).astype(jnp.bfloat16),
            preferred_element_type=jnp.float32,
        )
        bounds[0] = starts
        bounds[1] = starts + functions

    @pl.when(home)
    def _():
        pl.semaphore_wait(barrier, 26 + 2 + 7 + n_row - 1 + members - 1)

    @pl.when(jnp.logical_not(home))
    def _():
        device = (row, home_col, home_layer)
        pl.semaphore_signal(barrier, inc=1, device_id=device, device_id_type=MESH)
        pl.semaphore_wait(barrier, 26 + 2 + 7 + n_row - 1)

    def piece_copy(kind, target_layer, start):
        slot = dens.at[kind * n_col + col, pl.ds(slab * (target_layer % 2), slab)]
        source = density_ref.at[pl.ds(slab * (target_layer % 2), slab)]
        sent, got = sem_piece.at[target_layer], got_slab.at[kind * n_col + col]
        here = layer == target_layer
        far = remote(source, slot, sent, got, (row, col, target_layer))
        if start:
            when(here, pltpu.make_async_copy(source, slot, got).start)
        when(jnp.logical_not(here), far.start if start else far.wait_send)

    def strip_copy(kind, target, start):
        other, ll = target
        xx = (x + other) % 2
        slot = marg.at[kind * n_row + row]
        source = margin_ref.at[:, pl.ds(strip * ll, strip)]
        sent, got = sem_strip.at[ll * 2 + other], got_strip.at[kind * n_row + row]
        here = (layer == ll) & (other == 0)
        far = remote(source, slot, sent, got, (2 * y + xx, col, ll))
        if start and other == 0:
            when(here, pltpu.make_async_copy(source, slot, got).start)
        when(jnp.logical_not(here), far.start if start else far.wait_send)

    def first_copies(start):
        for kind in range(2):

            def pieces(kind=kind):
                for ll in (2, 3, 0, 1):
                    piece_copy(kind, ll, start)

            def strips(kind=kind):
                for target in plane:
                    strip_copy(kind, target, start)

            when((layer == kind) & (col < cols_of[kind]), pieces)
            when((layer == kind) & (row < rows_of[kind]) & live, strips)

    def around_copy(index):
        dr, dc, dl = shifts[index]
        return remote(
            near_ref, around.at[26 - index], sem_around.at[index], got_around.at[26 - index],
            shifted(shifts[index]),
        )

    def slab_of(kind, origin, half):
        return dens.at[kind * n_col + origin, pl.ds(pl.multiple_of(slab * half, slab), slab)]

    def ring_copy(kind, origin, way, step):
        block = slab_of(kind, origin, part)
        return remote(
            block, block, sem_ring.at[kind, way, step], got_slab.at[kind * n_col + origin],
            (onward, back)[way],
        )

    def pair_copy(kind, origin):
        block = slab_of(kind, origin, part)
        return remote(
            block, block, sem_pair.at[kind * n_col + origin],
            got_pair.at[kind * n_col + origin], partner,
        )

    def pair_wait(kind, origin):
        block = slab_of(kind, origin, 1 - part)
        remote(
            block, block, sem_pair.at[kind * n_col + origin],
            got_pair.at[kind * n_col + origin], partner,
        ).wait_recv()

    def ring_step(step, start):
        half = n_col // 2
        for way in ((0, 1) if step and step < half else (0,)):
            origin = (col + (n_col - step if way == 0 else step)) % n_col
            for kind in range(2):

                def body(kind=kind, origin=origin, way=way):
                    if start:
                        ring_copy(kind, origin, way, 0).wait_recv()
                    sends = [pair_copy(kind, origin)]
                    if way == 0 and step < half:
                        sends.append(ring_copy(kind, origin, 0, step))
                    if step == 0 or (way == 1 and step < half - 1):
                        sends.append(ring_copy(kind, origin, 1, step))
                    for copy in reversed(sends):
                        if start:
                            copy.start()
                        else:
                            copy.wait_send()

                when(origin < cols_of[kind], body)

    def own_strip(kind, other, start):
        origin = 2 * y + (x + other) % 2
        block = marg.at[kind * n_row + origin]
        got = got_strip.at[kind * n_row + origin]

        def body():
            if start:
                remote(block, block, sem_y.at[kind, other, 0], got, up).wait_recv()
            for way in range(2):
                copy = remote(block, block, sem_y.at[kind, other, way], got, (up, down)[way])
                send = copy.start if start else copy.wait_send
                if kind == 1 and way == 1:
                    when(y == 0, send)
                else:
                    send()

        when(live & (origin < rows_of[kind]), body)

    def next_strip(kind, other, way, start):
        origin_y = (y + (3 if way == 0 else 1)) % 4
        origin = 2 * origin_y + (x + other) % 2
        whole = marg.at[kind * n_row + origin]
        block = marg.at[kind * n_row + origin, pl.ds(share // 2 * way, share // 2)]

        def body():
            if start:
                remote(
                    whole, whole, sem_y.at[kind, other, way],
                    got_strip.at[kind * n_row + origin], up,
                ).wait_recv()
            sent = sem_half.at[kind, other, way]
            if kind == 0:
                copy = remote(
                    block, block, sent, got_half.at[origin, way], (up, down)[way]
                )
                (copy.start if start else copy.wait_send)()
            else:
                copy = remote(
                    whole, whole, sent, got_strip.at[n_row + origin], (up, down)[way]
                )
                when(y == (2, 3)[way], copy.start if start else copy.wait_send)

        if kind == 0:
            when(live, body)
        elif way == 0:
            when(live & (origin_y < 2), body)
        else:
            when(live & (origin_y == 0), body)

    def far_strip(kind, xx):
        origin = 2 * ((y + 2) % 4) + xx

        def halves():
            for way in range(2):
                block = marg.at[origin, pl.ds(share // 2 * way, share // 2)]
                remote(
                    block, block, sem_half.at[kind, xx, way], got_half.at[origin, way], up
                ).wait_recv()

        def whole():
            block = marg.at[n_row + origin]
            remote(
                block, block, sem_half.at[kind, xx, 0], got_strip.at[n_row + origin], up
            ).wait_recv()

        if kind == 0:
            when(live, halves)
        else:
            when(live & (y >= 2), whole)

    def nexts(kind, other, start):
        for way in range(2):
            next_strip(kind, other, way, start)

    def relays_low(start):
        ring_step(0, start)
        own_strip(0, 0, start)
        own_strip(1, 0, start)
        ring_step(1, start)
        ring_step(2, start)
        nexts(0, 0, start)
        ring_step(3, start)
        ring_step(4, start)
        nexts(1, 0, start)
        ring_step(5, start)
        ring_step(6, start)
        own_strip(0, 1, start)
        ring_step(7, start)
        ring_step(8, start)
        own_strip(1, 1, start)
        nexts(0, 1, start)
        nexts(1, 1, start)

    def relays_high(start):
        ring_step(0, start)
        ring_step(1, start)
        own_strip(0, 1, start)
        ring_step(2, start)
        own_strip(0, 0, start)
        ring_step(3, start)
        own_strip(1, 1, start)
        ring_step(4, start)
        own_strip(1, 0, start)
        ring_step(5, start)
        ring_step(6, start)
        nexts(0, 1, start)
        ring_step(7, start)
        nexts(0, 0, start)
        ring_step(8, start)
        nexts(1, 1, start)
        nexts(1, 0, start)

    def relays(start):
        when(layer < 2, lambda: relays_low(start))
        when(layer >= 2, lambda: relays_high(start))

    def spread_copy(index):
        return remote(
            pops_home, pops_mine, sem_spread.at[index], got_mine,
            (row, index // n_layer, index % n_layer),
        )

    def row_copies(source):
        return [
            remote(
                source, pops_rows.at[row], sem_rows.at[step], got_rows.at[row],
                ((row + step) % n_row, col, layer),
            )
            for step in range(1, n_row)
        ]

    def spread_step(start):
        def body(step, carry):
            copy = spread_copy((col * n_layer + layer + step) % members)
            if start:
                copy.start()
            else:
                copy.wait_send()
            return carry

        lax.fori_loop(1, members, body, 0)

    first_copies(True)
    for index in range(27):
        if index != 13:
            around_copy(index).start()
    relays(True)
    for kind in range(2):
        for origin in range(cols_of[kind]):
            pair_wait(kind, origin)
    product_ref[...] = jnp.zeros_like(product_ref)

    def add_shares(offset):
        origin_y = (y + offset) % 4

        def add(kind):
            def add_share(xx, carry):
                j = kind * n_row + 2 * origin_y + xx
                for side in range(2):
                    product_ref[...] += jnp.dot(
                        dens[2 * j + side],
                        marg[j, pl.ds(share // 2 * side, share // 2)],
                        preferred_element_type=jnp.float32,
                    )
                return carry

            lax.fori_loop(0, 2, add_share, 0)

        when(live, lambda: add(0))
        coupled = (origin_y == 0) | ((origin_y == 1) & (y > 0))
        when(live & coupled, lambda: add(1))

    for offset in (0, 1, 3):
        add_shares(offset)
    for kind in range(2):
        for xx in range(2):
            far_strip(kind, xx)
    add_shares(2)

    @pl.when(home)
    def _():
        side = product_ref.shape
        here = lax.broadcasted_iota(jnp.int32, side, 0) == lax.broadcasted_iota(jnp.int32, side, 1)
        diagonal = jnp.sum(jnp.where(here, product_ref[...], 0.0), axis=1, keepdims=True)
        wide = (side[0], functions_ref.shape[1])
        function = lax.broadcasted_iota(jnp.int32, wide, 0) + row * side[0]
        function = function.astype(jnp.float32)
        member = (function >= bounds[0, 0:1, :]) & (function < bounds[1, 0:1, :])
        pops_home[...] = jnp.sum(jnp.where(member, diagonal, 0.0), axis=0, keepdims=True)

    for index in range(27):
        if index != 13:
            around_copy(26 - index).wait_recv()
            near_out[index] = around[index]
    near_out[13] = near_ref[...]

    @pl.when(home)
    def _():
        for copy in row_copies(pops_home):
            copy.start()
        spread_step(True)

    @pl.when(jnp.logical_not(home))
    def _():
        spread_copy(0).wait_recv()
        for copy in row_copies(pops_mine):
            copy.start()

    first_copies(False)
    for index in range(27):
        if index != 13:
            around_copy(index).wait_send()
    relays(False)
    for step in range(1, n_row):
        mate = (row + step) % n_row
        slot = pops_rows.at[mate]
        remote(slot, slot, sem_rows.at[0], got_rows.at[mate], (mate, col, layer)).wait_recv()

    @pl.when(home)
    def _():
        pops_out[...] = pops_home[...]
        spread_step(False)

    @pl.when(jnp.logical_not(home))
    def _():
        pops_out[...] = pops_mine[...]

    for step in range(1, n_row):
        pops_out[...] += pops_rows[(row + step) % n_row]
    for copy in row_copies(pops_mine):
        copy.wait_send()


def gather_product(density, margin, functions, kind, offset, exponents):
    rows_here, piece_width = density.shape
    share, share_cols = margin.shape
    n_row, n_col, n_layer = (lax.axis_size(axis) for axis in ("row", "col", "layer"))
    depth = n_row * rows_here + REACH * BLK
    strip = share_cols // n_layer
    dma = pltpu.SemaphoreType.DMA
    near, atoms = (1, 128), functions.shape[0]
    vmem = pl.BlockSpec(memory_space=pltpu.VMEM)
    smem = pl.BlockSpec(memory_space=pltpu.SMEM)
    anywhere = pl.BlockSpec(memory_space=pl.ANY)
    pieces, shares = depth // piece_width, depth // share
    return pl.pallas_call(
        gather_kernel,
        out_shape=(
            jax.ShapeDtypeStruct((rows_here, strip), jnp.float32),
            jax.ShapeDtypeStruct((27,) + near, jnp.float32),
            jax.ShapeDtypeStruct((1, atoms), jnp.float32),
        ),
        in_specs=[anywhere, anywhere, vmem, smem, smem, smem],
        out_specs=(vmem, vmem, vmem),
        scratch_shapes=[
            pltpu.VMEM((pieces, rows_here, piece_width), jnp.bfloat16),
            pltpu.VMEM((shares, share, strip), jnp.bfloat16),
            pltpu.VMEM((27,) + near, jnp.float32),
            pltpu.VMEM(near, jnp.float32),
            pltpu.VMEM((2, 8, atoms), jnp.float32),
            pltpu.VMEM((1, atoms), jnp.float32),
            pltpu.VMEM((1, atoms), jnp.float32),
            pltpu.VMEM((n_row, 1, atoms), jnp.float32),
            dma((n_col * n_layer,)),
            dma,
            dma((n_row,)),
            dma((n_row,)),
            dma((27,)),
            dma((27,)),
            dma((n_layer,)),
            dma((2, 2, n_col // 2)),
            dma((pieces,)),
            dma((pieces,)),
            dma((pieces,)),
            dma((2 * n_layer,)),
            dma((2, 2, 2)),
            dma((2, 2, 2)),
            dma((shares,)),
            dma((n_row, 2)),
        ],
        compiler_params=pltpu.CompilerParams(
            collective_id=1, has_side_effects=True, vmem_limit_bytes=24 * 1024 * 1024
        ),
    )(density, margin, functions.reshape(1, -1), kind, offset, exponents)


def near_profile(cells, tile_of, extent, offset, exponent_of):
    local = jnp.arange(cells, dtype=jnp.int32)[None, :] - tile_of[:, None] * extent
    distance = local.astype(jnp.float32) - offset[:, None]
    return jnp.where(
        jnp.abs(distance) <= HALO, jnp.exp(-exponent_of[:, None] * distance * distance), 0.0
    )


def collocate(near, weights):
    index = jnp.arange(27, dtype=jnp.int32)
    exponent_of = near[:, 0]
    along_x = near_profile(TX, index % 3 - 1, TX, near[:, 1], exponent_of)
    along_y = near_profile(TY, index // 3 % 3 - 1, TY, near[:, 2], exponent_of)
    along_z = near_profile(TZ, index // 9 - 1, TZ, near[:, 3], exponent_of)
    paired = (weights[:, None] * along_x)[:, :, None] * along_y[:, None, :]
    return jnp.einsum("axy,az->xyz", paired, along_z, precision=lax.Precision.HIGHEST)


def shards(density, margin, block_pattern, atom_functions, atom_kind, atom_offset, exponents):
    rows_here, piece_width = density.shape
    share_rows, share_cols = margin.shape
    n_row = lax.axis_size("row")
    n_col = lax.axis_size("col")
    n_layer = lax.axis_size("layer")
    row_index = lax.axis_index("row")
    col_index = lax.axis_index("col")
    layer_index = lax.axis_index("layer")
    density_mask = lax.dynamic_slice(
        block_pattern,
        (row_index * (rows_here // BLK), (layer_index * n_col + col_index) * piece_width // BLK),
        (rows_here // BLK, piece_width // BLK),
    )
    masked = apply_pattern(density, density_mask)
    margin_mask = lax.dynamic_slice(
        block_pattern,
        ((layer_index * n_row + row_index) * share_rows // BLK, col_index * share_cols // BLK),
        (share_rows // BLK, share_cols // BLK),
    )
    margin_masked = apply_pattern(margin, margin_mask)
    product, near_all, pops = gather_product(
        masked, margin_masked, atom_functions, atom_kind, atom_offset, exponents
    )
    near = near_all[:, 0, :4]
    all_pop = pops.reshape(-1)
    index = jnp.arange(27, dtype=jnp.int32)
    near_atom = (
        ((row_index + index % 3 - 1) % n_row) * n_col + (col_index + index // 3 % 3 - 1) % n_col
    ) * n_layer + (layer_index + index // 9 - 1) % n_layer
    atoms = jnp.arange(all_pop.shape[0], dtype=jnp.int32)
    weights = jnp.sum(jnp.where(near_atom[:, None] == atoms[None, :], all_pop[None, :], 0.0), axis=1)
    return (product.astype(jnp.bfloat16), collocate(near, weights))


def apply_pattern(matrix, pattern_part):
    row_blocks = matrix.shape[0] // BLK
    col_blocks = matrix.shape[1] // BLK
    shaped = matrix.reshape(row_blocks, BLK, col_blocks, BLK)
    gate_mask = pattern_part.astype(jnp.bfloat16)
    return (shaped * gate_mask[:, None, :, None]).reshape(matrix.shape)


def shards(density, margin, block_pattern, atom_functions, atom_kind, atom_offset, exponents):
    rows_here, piece_width = density.shape
    share_rows, share_cols = margin.shape
    n_row = lax.axis_size("row")
    n_col = lax.axis_size("col")
    n_layer = lax.axis_size("layer")
    row_index = lax.axis_index("row")
    col_index = lax.axis_index("col")
    layer_index = lax.axis_index("layer")
    density_mask = lax.dynamic_slice(
        block_pattern,
        (row_index * (rows_here // BLK), (layer_index * n_col + col_index) * piece_width // BLK),
        (rows_here // BLK, piece_width // BLK),
    )
    masked = apply_pattern(density, density_mask)
    margin_mask = lax.dynamic_slice(
        block_pattern,
        ((layer_index * n_row + row_index) * share_rows // BLK, col_index * share_cols // BLK),
        (share_rows // BLK, share_cols // BLK),
    )
    margin_masked = apply_pattern(margin, margin_mask)
    product, near_all, pops = gather_product(
        masked, margin_masked, atom_functions, atom_kind, atom_offset, exponents
    )
    near = near_all[:, 0, :4]
    all_pop = pops.reshape(-1)
    index = jnp.arange(27, dtype=jnp.int32)
    near_atom = (
        ((row_index + index % 3 - 1) % n_row) * n_col + (col_index + index // 3 % 3 - 1) % n_col
    ) * n_layer + (layer_index + index // 9 - 1) % n_layer
    atoms = jnp.arange(all_pop.shape[0], dtype=jnp.int32)
    weights = jnp.sum(jnp.where(near_atom[:, None] == atoms[None, :], all_pop[None, :], 0.0), axis=1)
    return (product.astype(jnp.bfloat16), collocate(near, weights))


def apply_pattern(matrix, pattern_part):
    row_blocks = matrix.shape[0] // BLK
    col_blocks = matrix.shape[1] // BLK
    shaped = matrix.reshape(row_blocks, BLK, col_blocks, BLK)
    gate_mask = pattern_part.astype(jnp.bfloat16)
    return (shaped * gate_mask[:, None, :, None]).reshape(matrix.shape)


def kind_exponent(kinds_of, exponents):
    kind_match = kinds_of[:, None] == jnp.arange(exponents.shape[0], dtype=jnp.int32)[None, :]
    return jnp.sum(jnp.where(kind_match, exponents[None, :], 0.0), axis=1)


def solution(mesh):
    placed = (
        P("row", ("layer", "col")),
        P(("layer", "row"), "col"),
        P(),
        P(),
        P(("row", "col", "layer")),
        P(None, ("row", "col", "layer")),
        P(),
    )
    return jax.shard_map(
        shards,
        mesh=mesh,
        in_specs=placed,
        out_specs=(P("row", ("col", "layer")), P("row", "col", "layer")),
        check_vma=False,
    )
```
